128 devices in a mesh: rcv: 8 (over x_hi, z), src: 16 (over y, x_lo, core).
Axes of the slice: x: 4 (x_hi: 2, x_lo: 2; x = x_hi * 2 + x_lo), y: 4, z: 4, core: 2. Of those that a mesh axis runs over, the one named last changes fastest.
Arguments:
- reflection: bfloat16 [2, 16384, 16384], P(None, 'rcv', 'src'), may hold values from -6 to 6
- green: bfloat16 [2, 16384, 512], P(None, 'rcv', 'src'), may hold values from -0.046875 to 0.046875
- tile_mask: int32 [64, 64], replicated, may hold values from 0 to 1, as said below
- reference_index: int32 [512], P(('rcv', 'src')), may hold values from 0 to 511
Outputs:
- aligned: float32 [512, 2, 512], P(('rcv', 'src'))
The draws below stay inside these ranges and needn't reach their ends.
Inputs may be any that keep to these rules, and one draw needn't show every extreme that they name: `tile_mask`: entries below the diagonal are 0.
All inputs are finite; a program needn't handle non-finite values.
Results may differ from the reference program's by a relative error of at most 0.02.
Values may be sent and summed in bfloat16 or wider, within the bound.
No kernel may reach another device: no remote copies, remote signals or barrier semaphores. Data moves between devices by JAX's collectives and lax.ppermute only.
A program may use at most 128 MiB of HBM per device.

```python
import jax
import jax.numpy as jnp
from jax import lax

S = 16384
P_SIZE = 512
TILE = 256
TILES = 64
N_RCV = 8


def draw_tile_mask(key, part):
    levels = jax.random.randint(jax.random.fold_in(key, 17), (TILES, TILES), 0, 4)
    upper = jnp.arange(TILES)[:, None] <= jnp.arange(TILES)[None, :]
    return ((levels > 0) & upper).astype(jnp.int32)


def place_ends(result, stream_key, low, top_value):
    longest = result.shape.index(max(result.shape))
    spots = []
    for shift in (0, 1):
        where = [jax.random.randint(jax.random.fold_in(stream_key, axis), (), 0, length) for axis, length in enumerate(result.shape)]
        where[longest] = (where[longest] + shift) % result.shape[longest]
        spots.append(tuple(where))
    return result.at[spots[0]].set(low).at[spots[1]].set(top_value)


def block_levels(stream_key, extent, split, least, top_value):
    gain, own = 1.0, jax.random.fold_in(stream_key, 6)
    for dim, blocks in split:
        draws = jnp.exp(jax.random.uniform(jax.random.fold_in(own, dim), (blocks,), jnp.float32, least / len(split), top_value / len(split)))
        gain = gain * jnp.repeat(draws, extent[dim] // blocks).reshape([-1 if axis == dim else 1 for axis in range(len(extent))])
    return gain


def bell_draw(stream_key, shape, spread, reach, pieces=(), held_as=jnp.bfloat16):
    drawn = jax.random.normal(stream_key, shape, jnp.float32) * spread
    if len(pieces) > 0:
        drawn = block_levels(stream_key, shape, pieces, -0.22, 0.18) * drawn
    return jnp.clip(drawn, min=-reach, max=reach).astype(held_as)


def setup_inputs(seed: int = 0) -> dict:
    key_of = jax.random.split(jax.random.key(seed), 5)
    return {
        "reflection": bell_draw(key_of[0], (2, S, S), 1.0, 6.0, ((1, 8), (2, 16))),
        "green": bell_draw(key_of[1], (2, S, P_SIZE), S ** -0.5, 0.046875, ((1, 8), (2, 16))),
        "tile_mask": draw_tile_mask(jax.random.fold_in(key_of[4], 71), 0),
        "reference_index": place_ends(jax.random.randint(key_of[3], (P_SIZE,), 0, P_SIZE), jax.random.fold_in(key_of[3], 1), 0, P_SIZE - 1).astype(jnp.int32),
    }


exact_mode = lax.Precision.HIGHEST


def across(first, second):
    return lax.dot_general(first, second, (((0,), (0,)), ((), ())), preferred_element_type=jnp.float32)


def matmul(first, second):
    return jnp.dot(first, second, precision=exact_mode, preferred_element_type=jnp.float32)


def settle(value):
    return lax.optimization_barrier(value.astype(jnp.bfloat16)).astype(jnp.float32)


def reference(reflection, green, tile_mask, reference_index):
    block_rows = S // N_RCV
    tile_rows = block_rows // TILE
    col_tiles = jnp.arange(S // TILE)
    zero_value = jnp.zeros((), jnp.bfloat16)
    front_real = jnp.zeros((P_SIZE, S), jnp.float32)
    front_imag = jnp.zeros((P_SIZE, S), jnp.float32)
    back_real = jnp.zeros((P_SIZE, S), jnp.float32)
    back_imag = jnp.zeros((P_SIZE, S), jnp.float32)
    for block_index in range(N_RCV):
        row_start = block_index * block_rows
        measured = reflection[:, row_start:row_start + block_rows, :]
        tile_block = tile_mask[block_index * tile_rows:(block_index + 1) * tile_rows, :]
        row_tiles = block_index * tile_rows + jnp.arange(tile_rows)
        kept_tiles = tile_block == 1
        off_diag = kept_tiles & (row_tiles[:, None] != col_tiles[None, :])
        shaped = measured.reshape(2, tile_rows, TILE, S // TILE, TILE)
        acquired = jnp.where(kept_tiles[None, :, None, :, None], shaped, zero_value).reshape(2, block_rows, S)
        mirror_part = jnp.where(off_diag[None, :, None, :, None], shaped, zero_value).reshape(2, block_rows, S)
        green_real = green[0, row_start:row_start + block_rows, :]
        green_imag = green[1, row_start:row_start + block_rows, :]
        front_real = front_real + settle(across(green_real, acquired[0]) + across(green_imag, acquired[1]))
        front_imag = front_imag + settle(across(green_real, acquired[1]) - across(green_imag, acquired[0]))
        back_real = back_real + settle(across(green_real, mirror_part[0]) - across(green_imag, mirror_part[1]))
        back_imag = back_imag + settle(across(green_real, mirror_part[1]) + across(green_imag, mirror_part[0]))
    full_real = green[0].astype(jnp.float32)
    full_imag = green[1].astype(jnp.float32)
    focal_real = matmul(front_real, full_real) - matmul(front_imag, full_imag)
    focal_real = focal_real + (matmul(back_real, full_real) + matmul(back_imag, full_imag)).T
    focal_imag = matmul(front_real, full_imag) + matmul(front_imag, full_real)
    focal_imag = focal_imag + (matmul(back_imag, full_real) - matmul(back_real, full_imag)).T
    chosen = jnp.arange(P_SIZE).astype(jnp.int32)[None, :] == reference_index.astype(jnp.int32)[:, None]
    anchor_real = jnp.sum(jnp.where(chosen, focal_real, 0.0), axis=1)[:, None]
    anchor_imag = jnp.sum(jnp.where(chosen, focal_imag, 0.0), axis=1)[:, None]
    out_real = focal_real * anchor_real + focal_imag * anchor_imag
    out_imag = focal_imag * anchor_real - focal_real * anchor_imag
    return jnp.stack([out_real, out_imag], axis=1)
```

```python
import jax
import jax.numpy as jnp
from jax import lax
from jax.experimental import pallas as pl
from jax.experimental.pallas import tpu as pltpu
from jax.sharding import Mesh, PartitionSpec as P

P_SIZE = 512
TILE = 256
PARTS = (("xh", 2), ("z", 4), ("y", 4), ("xl", 2), ("core", 2))
RCV = ("xh", "z")
SRC = ("y", "xl", "core")
ALL = RCV + SRC
CHIPS = RCV + SRC[:2]
ROWS = 2048
COLS = 1024
ROW_TILES = ROWS // TILE
COL_TILES = COLS // TILE
SHARD = 32
N_CHIPS = 64
SWAP = [(0, 1), (1, 0)]


def place(xh, z, y, xl, core):
    return (((xh * 4 + z) * 4 + y) * 2 + xl) * 2 + core


def crossing(cross):
    return [
        (place(xh, z, y, xl, core), place(xl, y, 2 * xh + z // 2, z % 2, core ^ cross))
        for xh in range(2)
        for z in range(4)
        for y in range(4)
        for xl in range(2)
        for core in range(2)
    ]


def ring(step):
    return [(i, (i + step) % 4) for i in range(4)]


def dot(a, b):
    return lax.dot_general(a, b, (((1,), (0,)), ((), ())), preferred_element_type=jnp.float32)


def dot_nt(a, b):
    return lax.dot_general(a, b, (((1,), (1,)), ((), ())), preferred_element_type=jnp.float32)


def project_kernel(st, gk, a, out, gbuf, abuf, obuf, real_acc, imag_acc, gsem, asem, osem):
    half = P_SIZE

    def g_copy(r):
        return pltpu.make_async_copy(
            gk.at[:, pl.ds(r * TILE, TILE)], gbuf.at[:, pl.ds(r * TILE, TILE)], gsem.at[r]
        )

    def a_copy(c):
        return pltpu.make_async_copy(a.at[:, :, pl.ds(c * TILE, TILE)], abuf.at[c], asem.at[c])

    def o_copy(c):
        return pltpu.make_async_copy(
            obuf.at[:, :, pl.ds(c * TILE, TILE)], out.at[:, :, pl.ds(c * TILE, TILE)], osem.at[c]
        )

    @pl.when(st[32] != 0)
    def _():
        a_copy(0).start()
        for r in range(ROW_TILES):
            g_copy(r).start()
        for c in range(1, COL_TILES):
            a_copy(c).start()
        for r in range(ROW_TILES):
            g_copy(r).wait()

        def column(c, carry):
            a_copy(c).wait()
            real_acc[...] = jnp.zeros_like(real_acc)
            imag_acc[...] = jnp.zeros_like(imag_acc)
            lanes = pl.ds(pl.multiple_of(c * TILE, TILE), TILE)
            for r in range(ROW_TILES):

                @pl.when(st[r * COL_TILES + c] == 1)
                def _():
                    g = gbuf[:, r * TILE : (r + 1) * TILE]
                    real_acc[...] += dot(g, abuf[c, 0, r * TILE : (r + 1) * TILE, :])
                    imag_acc[...] += dot(g, abuf[c, 1, r * TILE : (r + 1) * TILE, :])

            obuf[2, :, lanes] = (real_acc[:half] - imag_acc[half:]).astype(jnp.bfloat16)
            obuf[3, :, lanes] = (imag_acc[:half] + real_acc[half:]).astype(jnp.bfloat16)

            @pl.when(st[36 + c] == 1)
            def _():
                rows = pl.ds(pl.multiple_of(st[40 + c] * TILE, TILE), TILE)
                g = gbuf[:, rows]
                real_acc[...] += dot(g, abuf[c, 0, rows, :])
                imag_acc[...] += dot(g, abuf[c, 1, rows, :])

            obuf[0, :, lanes] = (real_acc[:half] + imag_acc[half:]).astype(jnp.bfloat16)
            obuf[1, :, lanes] = (imag_acc[:half] - real_acc[half:]).astype(jnp.bfloat16)
            return carry

        lax.fori_loop(0, COL_TILES, column, 0)
        for c in range(COL_TILES):
            o_copy(c).start()
        for c in range(COL_TILES):
            o_copy(c).wait()


def focus_kernel(st, fb, own, near, after, before, far_a, far_b, keep, send, fbuf, gbuf, acc_r, acc_i, fsem, gsem):
    core = st[33]
    xh = st[34]
    z = st[35]

    def f_copy(c):
        return pltpu.make_async_copy(
            fb.at[:, :, pl.ds(c * TILE, TILE)], fbuf.at[:, :, pl.ds(c * TILE, TILE)], fsem.at[c]
        )

    def g_copies():
        copies = []

        def add(ref, x_other, z_step, part):
            block = 2 * ((z + z_step + 4) % 4) + (1 - xh if x_other else xh)
            slot = core if part == 0 else 1 - core
            row = pl.multiple_of(block * 64 + slot * SHARD, SHARD)
            copies.append(
                pltpu.make_async_copy(ref, gbuf.at[:, pl.ds(row, SHARD), :], gsem.at[len(copies)])
            )

        for part in range(2):
            add(own.at[part], False, 0, part)
            add(near.at[part], True, 0, part)
        for x_other in range(2):
            for part in range(2):
                add(after.at[x_other, part], x_other, -1, part)
                add(before.at[x_other, part], x_other, 1, part)
        for x_other in range(2):
            add(far_a.at[x_other], x_other, 2, 0)
            add(far_b.at[x_other], x_other, 2, 1)
        return copies

    sub = lax.broadcasted_iota(jnp.int32, (N_CHIPS, 8, P_SIZE), 1)
    low = sub < 4

    @pl.when(st[32] != 0)
    def _():
        copies = g_copies()
        for copy in copies:
            copy.start()
        for c in range(COL_TILES):
            f_copy(c).start()
        for copy in copies:
            copy.wait()
        for c in range(COL_TILES):
            f_copy(c).wait()
            cols = slice(c * TILE, (c + 1) * TILE)
            gr = gbuf[0, :, cols]
            gi = gbuf[1, :, cols]
            br = fbuf[2, :, cols]
            bi = fbuf[3, :, cols]
            left = jnp.concatenate([fbuf[0, :, cols], fbuf[1, :, cols], gr, gi], axis=1)
            right_r = jnp.concatenate([gr, -gi, br, bi], axis=1)
            right_i = jnp.concatenate([gi, gr, bi, -br], axis=1)
            if c == 0:
                acc_r[...] = dot_nt(left, right_r)
                acc_i[...] = dot_nt(left, right_i)
            else:
                acc_r[...] += dot_nt(left, right_r)
                acc_i[...] += dot_nt(left, right_i)
        re = acc_r[...].reshape(N_CHIPS, 8, P_SIZE)
        im = acc_i[...].reshape(N_CHIPS, 8, P_SIZE)
        first = jnp.where(low, re, pltpu.roll(im, 4, 1)).astype(jnp.bfloat16)
        second = jnp.where(low, pltpu.roll(re, 4, 1), im).astype(jnp.bfloat16)

        @pl.when(core == 0)
        def _():
            keep[...] = first
            send[...] = second

        @pl.when(core != 0)
        def _():
            keep[...] = second
            send[...] = first

    @pl.when(st[32] == 0)
    def _():
        keep[...] = jnp.zeros_like(keep)
        send[...] = jnp.zeros_like(send)


def align_kernel(index, parts, out):
    total = jnp.sum(parts[...].astype(jnp.float32), axis=0)
    lane = lax.broadcasted_iota(jnp.int32, (1, P_SIZE), 1)
    for i in range(4):
        re = total[i : i + 1]
        im = total[4 + i : 5 + i]
        chosen = lane == index[i]
        anchor_re = jnp.sum(jnp.where(chosen, re, 0.0), axis=1, keepdims=True)
        anchor_im = jnp.sum(jnp.where(chosen, im, 0.0), axis=1, keepdims=True)
        out[i, 0:1, :] = re * anchor_re + im * anchor_im
        out[i, 1:2, :] = im * anchor_re - re * anchor_im


def any_spec():
    return pl.BlockSpec(memory_space=pl.ANY)


def smem_spec():
    return pl.BlockSpec(memory_space=pltpu.SMEM)


def vmem_spec():
    return pl.BlockSpec(memory_space=pltpu.VMEM)


def tile_states(tile_mask):
    rcv = lax.axis_index(RCV)
    src = lax.axis_index(SRC)
    tiles = lax.dynamic_slice(tile_mask, (rcv * ROW_TILES, src * COL_TILES), (ROW_TILES, COL_TILES))
    kept = (tiles == 1).astype(jnp.int32)
    rows = jnp.arange(ROW_TILES)[:, None] + rcv * ROW_TILES
    cols = jnp.arange(COL_TILES)[None, :] + src * COL_TILES
    diag = (rows == cols).astype(jnp.int32)
    state = kept * (1 + diag)
    diag_row = jnp.clip(cols[0] - rcv * ROW_TILES, 0, ROW_TILES - 1)
    diag_on = jnp.max(kept * diag, axis=0)
    scalars = jnp.stack(
        [jnp.max(kept), lax.axis_index("core"), lax.axis_index("xh"), lax.axis_index("z")]
    )
    return jnp.concatenate([state.reshape(-1), scalars, diag_on, diag_row]).astype(jnp.int32)


def body(reflection, green, tile_mask, reference_index):
    lines = jnp.transpose(green, (0, 2, 1))
    gathered = lax.all_gather(lines, SRC, axis=1, tiled=True)
    state = tile_states(tile_mask)
    core = lax.axis_index("core")
    mid = ROWS // 2
    same = lax.dynamic_slice_in_dim(lines, core * mid, mid, 2)
    other = lax.dynamic_slice_in_dim(lines, (1 - core) * mid, mid, 2)
    own = jnp.stack([lax.ppermute(same, ALL, crossing(0)), lax.ppermute(other, ALL, crossing(1))])
    near = lax.ppermute(own, "xh", SWAP)
    pair = jnp.stack([own, near])
    after = lax.ppermute(pair, "z", ring(1))
    before = lax.ppermute(pair, "z", ring(-1))
    far_a = lax.ppermute(after[:, 0], "z", ring(1))
    far_b = lax.ppermute(before[:, 1], "z", ring(-1))

    fb = pl.pallas_call(
        project_kernel,
        out_shape=jax.ShapeDtypeStruct((4, P_SIZE, COLS), jnp.bfloat16),
        in_specs=[smem_spec(), any_spec(), any_spec()],
        out_specs=any_spec(),
        scratch_shapes=[
            pltpu.VMEM((2 * P_SIZE, ROWS), jnp.bfloat16),
            pltpu.VMEM((COL_TILES, 2, ROWS, TILE), jnp.bfloat16),
            pltpu.VMEM((4, P_SIZE, COLS), jnp.bfloat16),
            pltpu.VMEM((2 * P_SIZE, TILE), jnp.float32),
            pltpu.VMEM((2 * P_SIZE, TILE), jnp.float32),
            pltpu.SemaphoreType.DMA((ROW_TILES,)),
            pltpu.SemaphoreType.DMA((COL_TILES,)),
            pltpu.SemaphoreType.DMA((COL_TILES,)),
        ],
        compiler_params=pltpu.CompilerParams(vmem_limit_bytes=40 << 20),
        cost_estimate=pl.CostEstimate(flops=8 << 30, transcendentals=0, bytes_accessed=16 << 20),
        name="project",
    )(state, gathered.reshape(2 * P_SIZE, ROWS), reflection)

    block = jax.ShapeDtypeStruct((N_CHIPS, 8, P_SIZE), jnp.bfloat16)
    keep, send = pl.pallas_call(
        focus_kernel,
        out_shape=(block, block),
        in_specs=[smem_spec()] + [any_spec()] * 7,
        out_specs=(vmem_spec(), vmem_spec()),
        scratch_shapes=[
            pltpu.VMEM((4, P_SIZE, COLS), jnp.bfloat16),
            pltpu.VMEM((2, P_SIZE, COLS), jnp.bfloat16),
            pltpu.VMEM((P_SIZE, P_SIZE), jnp.float32),
            pltpu.VMEM((P_SIZE, P_SIZE), jnp.float32),
            pltpu.SemaphoreType.DMA((COL_TILES,)),
            pltpu.SemaphoreType.DMA((16,)),
        ],
        compiler_params=pltpu.CompilerParams(vmem_limit_bytes=40 << 20),
        cost_estimate=pl.CostEstimate(flops=4 << 30, transcendentals=0, bytes_accessed=8 << 20),
        name="focus",
    )(state, fb, own, near, after, before, far_a, far_b)
    taken = lax.ppermute(send, "core", SWAP)
    summed = (keep.astype(jnp.float32) + taken.astype(jnp.float32)).astype(jnp.bfloat16)
    parts = lax.all_to_all(summed, CHIPS, 0, 0)
    return pl.pallas_call(
        align_kernel,
        out_shape=jax.ShapeDtypeStruct((4, 2, P_SIZE), jnp.float32),
        in_specs=[smem_spec(), vmem_spec()],
        out_specs=vmem_spec(),
        name="align",
    )(reference_index, parts)


def solution(mesh):
    fine = Mesh(mesh.devices.reshape([size for _, size in PARTS]), [name for name, _ in PARTS])
    return jax.shard_map(
        body,
        mesh=fine,
        in_specs=(P(None, RCV, SRC), P(None, RCV, SRC), P(), P(ALL)),
        out_specs=P(ALL, None, None),
        check_vma=False,
    )
```

```python
import jax
import jax.numpy as jnp
from jax import lax
from jax.experimental import pallas as pl
from jax.experimental.pallas import tpu as pltpu
from jax.sharding import Mesh, PartitionSpec as P

P_SIZE = 512
TILE = 256
PARTS = (("xh", 2), ("z", 4), ("y", 4), ("xl", 2), ("core", 2))
RCV = ("xh", "z")
SRC = ("y", "xl", "core")
ALL = RCV + SRC
CHIPS = RCV + SRC[:2]
ROWS = 2048
COLS = 1024
ROW_TILES = ROWS // TILE
COL_TILES = COLS // TILE
SHARD = 32
N_CHIPS = 64
SWAP = [(0, 1), (1, 0)]


def place(xh, z, y, xl, core):
    return (((xh * 4 + z) * 4 + y) * 2 + xl) * 2 + core


def crossing(cross):
    return [
        (place(xh, z, y, xl, core), place(xl, y, 2 * xh + z // 2, z % 2, core ^ cross))
        for xh in range(2)
        for z in range(4)
        for y in range(4)
        for xl in range(2)
        for core in range(2)
    ]


def ring(step):
    return [(i, (i + step) % 4) for i in range(4)]


def dot(a, b):
    return lax.dot_general(a, b, (((1,), (0,)), ((), ())), preferred_element_type=jnp.float32)


def dot_nt(a, b):
    return lax.dot_general(a, b, (((1,), (1,)), ((), ())), preferred_element_type=jnp.float32)


def project_kernel(st, own, after, before, far_a, far_b, swap, swap_far, a, out, gbuf, abuf, acc, gsem, asem):
    half = P_SIZE
    core = st[49]
    xl = st[52]
    y = st[53]
    mid = ROWS // 2

    def g_copies():
        copies = []

        def add(ref, x_other, y_step, other, lanes):
            line = 4 * ((y + y_step + 4) % 4) + 2 * (1 - xl if x_other else xl)
            row = pl.multiple_of((line + (1 - core if other else core)) * SHARD, SHARD)
            target = gbuf.at[:, pl.ds(row, SHARD), lanes]
            copies.append(pltpu.make_async_copy(ref, target, gsem.at[len(copies)]))

        whole = pl.ds(0, ROWS)
        low = pl.ds(0, mid)
        high = pl.ds(mid, mid)
        for x in range(2):
            add(own.at[x], x, 0, False, whole)
            add(after.at[x], x, -1, False, whole)
            add(before.at[x], x, 1, False, whole)
            add(far_a.at[x], x, 2, False, low)
            add(far_b.at[x], x, 2, False, high)
        for x in range(2):
            add(swap.at[0, x], x, 0, True, whole)
            add(swap.at[1, x], x, -1, True, whole)
            add(swap.at[2, x], x, 1, True, whole)
            add(swap_far.at[0, x], x, 2, True, low)
            add(swap_far.at[1, x], x, 2, True, high)
        return copies

    def a_copy(c, i):
        row = pl.multiple_of(st[8 + c * ROW_TILES + i] * TILE, TILE)
        return pltpu.make_async_copy(
            a.at[:, pl.ds(row, TILE), pl.ds(c * TILE, TILE)],
            abuf.at[c, :, pl.ds(i * TILE, TILE), :],
            asem.at[c, i],
        )

    def d_copy(c):
        row = pl.multiple_of(st[44 + c] * TILE, TILE)
        return pltpu.make_async_copy(
            a.at[:, pl.ds(row, TILE), pl.ds(c * TILE, TILE)],
            abuf.at[c, :, pl.ds(ROWS, TILE), :],
            asem.at[c, ROW_TILES],
        )

    @pl.when(st[48] != 0)
    def _():
        copies = g_copies()
        for copy in copies:
            copy.start()
        for c in range(COL_TILES):
            for i in range(ROW_TILES):

                @pl.when(i < st[c])
                def _():
                    a_copy(c, i).start()

            @pl.when(st[40 + c] != 0)
            def _():
                d_copy(c).start()

        for copy in copies:
            copy.wait()

        def column(c, carry):
            n = st[c]
            lanes = pl.ds(pl.multiple_of(c * TILE, TILE), TILE)

            def product(tiles, start):
                left = jnp.concatenate(
                    [
                        gbuf[:, :, pl.ds(pl.multiple_of(t * TILE, TILE), TILE)].reshape(2 * half, TILE)
                        for t in tiles
                    ],
                    axis=1,
                )
                rows = pl.ds(pl.multiple_of(start * TILE, TILE), len(tiles) * TILE)
                right = jnp.concatenate([abuf[c, 0, rows, :], abuf[c, 1, rows, :]], axis=1)
                return dot(left, right)

            def listed(first, count):
                return [st[8 + c * ROW_TILES + first + i] for i in range(count)]

            for i in range(ROW_TILES):

                @pl.when(i < n)
                def _():
                    a_copy(c, i).wait()

            @pl.when(n < 4)
            def _():
                acc[...] = jnp.zeros_like(acc)

            @pl.when(n >= 4)
            def _():
                acc[...] = product(listed(0, 4), 0)

            @pl.when(n == 8)
            def _():
                acc[...] += product(listed(4, 4), 4)

            @pl.when((n & 2) != 0)
            def _():
                first = n & 4
                acc[...] += product(listed(first, 2), first)

            @pl.when((n & 1) != 0)
            def _():
                acc[...] += product(listed(n - 1, 1), n - 1)

            out[2, :, lanes] = (acc[:half, :TILE] - acc[half:, TILE:]).astype(jnp.bfloat16)
            out[3, :, lanes] = (acc[:half, TILE:] + acc[half:, :TILE]).astype(jnp.bfloat16)

            @pl.when(st[40 + c] != 0)
            def _():
                d_copy(c).wait()
                acc[...] += product([st[44 + c]], ROW_TILES)

            out[0, :, lanes] = (acc[:half, :TILE] + acc[half:, TILE:]).astype(jnp.bfloat16)
            out[1, :, lanes] = (acc[:half, TILE:] - acc[half:, :TILE]).astype(jnp.bfloat16)
            return carry

        lax.fori_loop(0, COL_TILES, column, 0)


def focus_kernel(st, fb, own, near, after, before, near_after, near_before, far_a, far_b, keep, send, gbuf, acc, gsem):
    core = st[49]
    xh = st[50]
    z = st[51]

    def g_copies():
        copies = []

        def add(ref, x_other, z_step, part):
            block = 2 * ((z + z_step + 4) % 4) + (1 - xh if x_other else xh)
            slot = core if part == 0 else 1 - core
            row = pl.multiple_of(block * 64 + slot * SHARD, SHARD)
            copies.append(
                pltpu.make_async_copy(ref, gbuf.at[:, pl.ds(row, SHARD), :], gsem.at[len(copies)])
            )

        for part in range(2):
            add(own.at[part], False, 0, part)
            add(near.at[part], True, 0, part)
            add(after.at[part], False, -1, part)
            add(before.at[part], False, 1, part)
            add(near_after.at[part], True, -1, part)
            add(near_before.at[part], True, 1, part)
        for x_other in range(2):
            add(far_a.at[x_other], x_other, 2, 0)
            add(far_b.at[x_other], x_other, 2, 1)
        return copies

    sub = lax.broadcasted_iota(jnp.int32, (N_CHIPS, 8, P_SIZE), 1)
    low = sub < 4

    @pl.when(st[48] != 0)
    def _():
        copies = g_copies()
        for copy in copies:
            copy.start()
        for copy in copies:
            copy.wait()
        for c in range(COL_TILES):
            cols = slice(c * TILE, (c + 1) * TILE)
            gr = gbuf[0, :, cols]
            gi = gbuf[1, :, cols]
            fr = fb[0, :, cols]
            fi = fb[1, :, cols]
            left = jnp.concatenate(
                [
                    jnp.concatenate([fr, -fi, gr, gi], axis=1),
                    jnp.concatenate([fi, fr, -gi, gr], axis=1),
                ],
                axis=0,
            )
            right = jnp.concatenate([gr, gi, fb[2, :, cols], fb[3, :, cols]], axis=1)
            if c == 0:
                acc[...] = dot_nt(left, right)
            else:
                acc[...] += dot_nt(left, right)
        re = acc[:P_SIZE].reshape(N_CHIPS, 8, P_SIZE)
        im = acc[P_SIZE:].reshape(N_CHIPS, 8, P_SIZE)
        first = jnp.where(low, re, pltpu.roll(im, 4, 1)).astype(jnp.bfloat16)
        second = jnp.where(low, pltpu.roll(re, 4, 1), im).astype(jnp.bfloat16)

        @pl.when(core == 0)
        def _():
            keep[...] = first
            send[...] = second

        @pl.when(core != 0)
        def _():
            keep[...] = second
            send[...] = first

    @pl.when(st[48] == 0)
    def _():
        keep[...] = jnp.zeros_like(keep)
        send[...] = jnp.zeros_like(send)


def align_kernel(index, parts, out):
    total = jnp.sum(parts[...].astype(jnp.float32), axis=0)
    lane = lax.broadcasted_iota(jnp.int32, (1, P_SIZE), 1)
    for i in range(4):
        re = total[i : i + 1]
        im = total[4 + i : 5 + i]
        chosen = lane == index[i]
        anchor_re = jnp.sum(jnp.where(chosen, re, 0.0), axis=1, keepdims=True)
        anchor_im = jnp.sum(jnp.where(chosen, im, 0.0), axis=1, keepdims=True)
        out[i, 0:1, :] = re * anchor_re + im * anchor_im
        out[i, 1:2, :] = im * anchor_re - re * anchor_im


def any_spec():
    return pl.BlockSpec(memory_space=pl.ANY)


def hbm_spec():
    return pl.BlockSpec(memory_space=pltpu.HBM)


def smem_spec():
    return pl.BlockSpec(memory_space=pltpu.SMEM)


def vmem_spec():
    return pl.BlockSpec(memory_space=pltpu.VMEM)


def tile_states(tile_mask):
    rcv = lax.axis_index(RCV)
    src = lax.axis_index(SRC)
    tiles = lax.dynamic_slice(tile_mask, (rcv * ROW_TILES, src * COL_TILES), (ROW_TILES, COL_TILES))
    kept = (tiles == 1).T
    rows = jnp.arange(ROW_TILES)[None, :]
    diag_row = jnp.arange(COL_TILES)[:, None] + src * COL_TILES - rcv * ROW_TILES
    diag = rows == diag_row
    plain = (kept & ~diag).astype(jnp.int32)
    count = jnp.sum(plain, axis=1)
    before = jnp.sum(plain[:, None, :] * (rows[0][None, :] < rows[0][:, None]), axis=2)
    hit = (before[:, None, :] == rows[0][None, :, None]) & (plain[:, None, :] == 1)
    order = jnp.sum(jnp.where(hit, rows[0][None, None, :], 0), axis=2)
    diag_on = jnp.sum((kept & diag).astype(jnp.int32), axis=1)
    diag_at = jnp.clip(diag_row[:, 0], 0, ROW_TILES - 1)
    scalars = jnp.stack(
        [jnp.max(kept.astype(jnp.int32))] + [lax.axis_index(name) for name in ("core", "xh", "z", "xl", "y")]
    )
    return jnp.concatenate(
        [count, jnp.zeros((4,), jnp.int32), order.reshape(-1), diag_on, diag_at, scalars]
    ).astype(jnp.int32)


def body(reflection, green, tile_mask, reference_index):
    lines = jnp.transpose(green, (0, 2, 1))
    state = tile_states(tile_mask)
    core = lax.axis_index("core")
    mid = ROWS // 2

    beside = lax.ppermute(lines, "xl", SWAP)
    same = lax.dynamic_slice_in_dim(lines, core * mid, mid, 2)
    other = lax.dynamic_slice_in_dim(lines, (1 - core) * mid, mid, 2)
    part_a = lax.ppermute(same, ALL, crossing(0))
    part_b = lax.ppermute(other, ALL, crossing(1))

    g_own = jnp.stack([lines, beside])
    g_after = lax.ppermute(g_own, "y", ring(1))
    g_before = lax.ppermute(g_own, "y", ring(-1))
    own = jnp.stack([part_a, part_b])
    after = lax.ppermute(own, "z", ring(1))
    before = lax.ppermute(own, "z", ring(-1))
    near = lax.ppermute(own, "xh", SWAP)
    g_far_a = lax.ppermute(g_after[..., :mid], "y", ring(1))
    g_far_b = lax.ppermute(g_before[..., mid:], "y", ring(-1))
    swap = lax.ppermute(jnp.stack([g_own, g_after, g_before]), "core", SWAP)
    near_after = lax.ppermute(near, "z", ring(1))
    near_before = lax.ppermute(near, "z", ring(-1))
    swap_far = lax.ppermute(jnp.stack([g_far_a, g_far_b]), "core", SWAP)
    far_a = lax.ppermute(jnp.stack([after[0], near_after[0]]), "z", ring(1))
    far_b = lax.ppermute(jnp.stack([before[1], near_before[1]]), "z", ring(-1))

    fb = pl.pallas_call(
        project_kernel,
        out_shape=jax.ShapeDtypeStruct((4, P_SIZE, COLS), jnp.bfloat16),
        in_specs=[smem_spec()] + [any_spec()] * 7 + [hbm_spec()],
        out_specs=vmem_spec(),
        scratch_shapes=[
            pltpu.VMEM((2, P_SIZE, ROWS), jnp.bfloat16),
            pltpu.VMEM((COL_TILES, 2, ROWS + TILE, TILE), jnp.bfloat16),
            pltpu.VMEM((2 * P_SIZE, 2 * TILE), jnp.float32),
            pltpu.SemaphoreType.DMA((20,)),
            pltpu.SemaphoreType.DMA((COL_TILES, ROW_TILES + 1)),
        ],
        compiler_params=pltpu.CompilerParams(vmem_limit_bytes=44 << 20),
        cost_estimate=pl.CostEstimate(flops=8 << 30, transcendentals=0, bytes_accessed=16 << 20),
        name="project",
    )(state, g_own, g_after, g_before, g_far_a, g_far_b, swap, swap_far, reflection)

    block = jax.ShapeDtypeStruct((N_CHIPS, 8, P_SIZE), jnp.bfloat16)
    keep, send = pl.pallas_call(
        focus_kernel,
        out_shape=(block, block),
        in_specs=[smem_spec(), vmem_spec()] + [any_spec()] * 8,
        out_specs=(vmem_spec(), vmem_spec()),
        scratch_shapes=[
            pltpu.VMEM((2, P_SIZE, COLS), jnp.bfloat16),
            pltpu.VMEM((2 * P_SIZE, P_SIZE), jnp.float32),
            pltpu.SemaphoreType.DMA((16,)),
        ],
        compiler_params=pltpu.CompilerParams(vmem_limit_bytes=44 << 20),
        cost_estimate=pl.CostEstimate(flops=4 << 30, transcendentals=0, bytes_accessed=8 << 20),
        name="focus",
    )(state, fb, own, near, after, before, near_after, near_before, far_a, far_b)
    taken = lax.ppermute(send, "core", SWAP)
    summed = (keep.astype(jnp.float32) + taken.astype(jnp.float32)).astype(jnp.bfloat16)
    parts = lax.all_to_all(summed, CHIPS, 0, 0)
    return pl.pallas_call(
        align_kernel,
        out_shape=jax.ShapeDtypeStruct((4, 2, P_SIZE), jnp.float32),
        in_specs=[smem_spec(), vmem_spec()],
        out_specs=vmem_spec(),
        name="align",
    )(reference_index, parts)


def solution(mesh):
    fine = Mesh(mesh.devices.reshape([size for _, size in PARTS]), [name for name, _ in PARTS])
    return jax.shard_map(
        body,
        mesh=fine,
        in_specs=(P(None, RCV, SRC), P(None, RCV, SRC), P(), P(ALL)),
        out_specs=P(ALL, None, None),
        check_vma=False,
    )
```

```python
import jax
import jax.numpy as jnp
from jax import lax
from jax.experimental import pallas as pl
from jax.experimental.pallas import tpu as pltpu
from jax.sharding import Mesh, PartitionSpec as P

P_SIZE = 512
TILE = 256
PARTS = (("xh", 2), ("z", 4), ("y", 4), ("xl", 2), ("core", 2))
RCV = ("xh", "z")
SRC = ("y", "xl", "core")
ALL = RCV + SRC
CHIPS = RCV + SRC[:2]
ROWS = 2048
COLS = 1024
ROW_TILES = ROWS // TILE
COL_TILES = COLS // TILE
SHARD = 32
N_CHIPS = 64
SWAP = [(0, 1), (1, 0)]


def place(xh, z, y, xl, core):
    return (((xh * 4 + z) * 4 + y) * 2 + xl) * 2 + core


def crossing(cross):
    return [
        (place(xh, z, y, xl, core), place(xl, y, 2 * xh + z // 2, z % 2, core ^ cross))
        for xh in range(2)
        for z in range(4)
        for y in range(4)
        for xl in range(2)
        for core in range(2)
    ]


def ring(step):
    return [(i, (i + step) % 4) for i in range(4)]


def dot(a, b):
    return lax.dot_general(a, b, (((1,), (0,)), ((), ())), preferred_element_type=jnp.float32)


def dot_nt(a, b):
    return lax.dot_general(a, b, (((1,), (1,)), ((), ())), preferred_element_type=jnp.float32)


def load_kernel(st, a, abuf, asem):
    def tile_copy(c, source, i):
        row = pl.multiple_of(source * TILE, TILE)
        return pltpu.make_async_copy(
            a.at[:, pl.ds(row, TILE), pl.ds(c * TILE, TILE)],
            abuf.at[c, :, pl.ds(i * TILE, TILE), :],
            asem.at[c, i],
        )

    def visit(act):
        for c in range(COL_TILES):
            for i in range(ROW_TILES):

                @pl.when(i < st[c])
                def _():
                    act(tile_copy(c, st[8 + c * ROW_TILES + i], i))

            @pl.when(st[40 + c] != 0)
            def _():
                act(tile_copy(c, st[44 + c], ROW_TILES))

    visit(lambda copy: copy.start())
    visit(lambda copy: copy.wait())


def project(st, abuf, acc, fb, left_of, targets):
    def column(c, carry):
        n = st[c]
        lanes = pl.ds(pl.multiple_of(c * TILE, TILE), TILE)

        def product(tiles, start):
            left = jnp.concatenate([left_of(t) for t in tiles], axis=1)
            rows = pl.ds(pl.multiple_of(start * TILE, TILE), len(tiles) * TILE)
            right = jnp.concatenate([abuf[c, 0, rows, :], abuf[c, 1, rows, :]], axis=1)
            return dot(left, right)

        def listed(first, count):
            return [st[8 + c * ROW_TILES + first + i] for i in range(count)]

        @pl.when(n < 4)
        def _():
            acc[...] = jnp.zeros_like(acc)

        @pl.when(n >= 4)
        def _():
            acc[...] = product(listed(0, 4), 0)

        @pl.when(n == 8)
        def _():
            acc[...] += product(listed(4, 4), 4)

        @pl.when((n & 2) != 0)
        def _():
            first = n & 4
            acc[...] += product(listed(first, 2), first)

        @pl.when((n & 1) != 0)
        def _():
            acc[...] += product(listed(n - 1, 1), n - 1)

        def store(front, back):
            for b, row in enumerate(targets):
                rows = pl.ds(pl.multiple_of(row, SHARD), SHARD)
                at = 2 * SHARD * b
                rr = acc[at : at + SHARD, :TILE]
                ri = acc[at : at + SHARD, TILE:]
                ir = acc[at + SHARD : at + 2 * SHARD, :TILE]
                ii = acc[at + SHARD : at + 2 * SHARD, TILE:]
                if front:
                    fb[0, rows, lanes] = (rr + ii).astype(jnp.bfloat16)
                    fb[1, rows, lanes] = (ri - ir).astype(jnp.bfloat16)
                if back:
                    fb[2, rows, lanes] = (rr - ii).astype(jnp.bfloat16)
                    fb[3, rows, lanes] = (ri + ir).astype(jnp.bfloat16)

        @pl.when(st[40 + c] == 0)
        def _():
            store(True, True)

        @pl.when(st[40 + c] != 0)
        def _():
            store(False, True)
            acc[...] += product([st[44 + c]], ROW_TILES)
            store(True, False)

        return carry

    lax.fori_loop(0, COL_TILES, column, 0)


def line_row(st, x_other, y_step, other):
    core, xl, y = st[49], st[52], st[53]
    line = 4 * ((y + y_step + 4) % 4) + 2 * (1 - xl if x_other else xl)
    return (line + (1 - core if other else core)) * SHARD


def tile_lanes(t):
    return pl.ds(pl.multiple_of(t * TILE, TILE), TILE)


def near_kernel(st, abuf, own, after, before, fb, acc):
    @pl.when(st[48] != 0)
    def _():
        def left_of(t):
            return jnp.concatenate(
                [ref[:, :, :, tile_lanes(t)].reshape(4 * SHARD, TILE) for ref in (own, after, before)], axis=0
            )

        targets = [line_row(st, x, step, False) for step in (0, -1, 1) for x in range(2)]
        project(st, abuf, acc, fb, left_of, targets)


def swap_kernel(st, abuf, fb_in, swap, fb, acc):
    @pl.when(st[48] != 0)
    def _():
        def left_of(t):
            return swap[:, :, :, :, tile_lanes(t)].reshape(12 * SHARD, TILE)

        targets = [line_row(st, x, step, True) for step in (0, -1, 1) for x in range(2)]
        project(st, abuf, acc, fb, left_of, targets)


def finish_kernel(
    st, abuf, fb_in, g_far_a, g_far_b, swap_far,
    own, near, after, before, near_after, near_before, far_a, far_b,
    fb, keep, send, gbuf, acc, wide, gsem,
):
    core = st[49]
    xh = st[50]
    z = st[51]

    def g_copies():
        copies = []

        def add(ref, x_other, z_step, part):
            block = 2 * ((z + z_step + 4) % 4) + (1 - xh if x_other else xh)
            slot = core if part == 0 else 1 - core
            row = pl.multiple_of(block * 64 + slot * SHARD, SHARD)
            copies.append(
                pltpu.make_async_copy(ref, gbuf.at[:, pl.ds(row, SHARD), :], gsem.at[len(copies)])
            )

        for part in range(2):
            add(own.at[part], False, 0, part)
            add(near.at[part], True, 0, part)
            add(after.at[part], False, -1, part)
            add(before.at[part], False, 1, part)
            add(near_after.at[part], True, -1, part)
            add(near_before.at[part], True, 1, part)
            add(far_a.at[part], False, 2, part)
            add(far_b.at[part], True, 2, part)
        return copies

    sub = lax.broadcasted_iota(jnp.int32, (N_CHIPS, 8, P_SIZE), 1)
    low = sub < 4

    @pl.when(st[48] != 0)
    def _():
        copies = g_copies()
        for copy in copies:
            copy.start()

        def left_of(t):
            lanes = tile_lanes(t)
            return jnp.concatenate(
                [
                    g_far_a[:, :, lanes].reshape(2 * SHARD, TILE),
                    g_far_b[:, :, lanes].reshape(2 * SHARD, TILE),
                    swap_far[:, :, :, lanes].reshape(4 * SHARD, TILE),
                ],
                axis=0,
            )

        targets = [line_row(st, x, 2, other) for other in (False, True) for x in range(2)]
        project(st, abuf, acc, fb, left_of, targets)
        for copy in copies:
            copy.wait()
        for c in range(COL_TILES):
            cols = slice(c * TILE, (c + 1) * TILE)
            gr = gbuf[0, :, cols]
            gi = gbuf[1, :, cols]
            fr = fb[0, :, cols]
            fi = fb[1, :, cols]
            left = jnp.concatenate(
                [
                    jnp.concatenate([fr, -fi, gr, gi], axis=1),
                    jnp.concatenate([fi, fr, -gi, gr], axis=1),
                ],
                axis=0,
            )
            right = jnp.concatenate([gr, gi, fb[2, :, cols], fb[3, :, cols]], axis=1)
            if c == 0:
                wide[...] = dot_nt(left, right)
            else:
                wide[...] += dot_nt(left, right)
        re = wide[:P_SIZE].reshape(N_CHIPS, 8, P_SIZE)
        im = wide[P_SIZE:].reshape(N_CHIPS, 8, P_SIZE)
        first = jnp.where(low, re, pltpu.roll(im, 4, 1)).astype(jnp.bfloat16)
        second = jnp.where(low, pltpu.roll(re, 4, 1), im).astype(jnp.bfloat16)

        @pl.when(core == 0)
        def _():
            keep[...] = first
            send[...] = second

        @pl.when(core != 0)
        def _():
            keep[...] = second
            send[...] = first

    @pl.when(st[48] == 0)
    def _():
        keep[...] = jnp.zeros_like(keep)
        send[...] = jnp.zeros_like(send)


def align_kernel(index, parts, out):
    total = jnp.sum(parts[...].astype(jnp.float32), axis=0)
    lane = lax.broadcasted_iota(jnp.int32, (1, P_SIZE), 1)
    for i in range(4):
        re = total[i : i + 1]
        im = total[4 + i : 5 + i]
        chosen = lane == index[i]
        anchor_re = jnp.sum(jnp.where(chosen, re, 0.0), axis=1, keepdims=True)
        anchor_im = jnp.sum(jnp.where(chosen, im, 0.0), axis=1, keepdims=True)
        out[i, 0:1, :] = re * anchor_re + im * anchor_im
        out[i, 1:2, :] = im * anchor_re - re * anchor_im


def any_spec():
    return pl.BlockSpec(memory_space=pl.ANY)


def hbm_spec():
    return pl.BlockSpec(memory_space=pltpu.HBM)


def smem_spec():
    return pl.BlockSpec(memory_space=pltpu.SMEM)


def vmem_spec():
    return pl.BlockSpec(memory_space=pltpu.VMEM)


def tile_states(tile_mask):
    rcv = lax.axis_index(RCV)
    src = lax.axis_index(SRC)
    tiles = lax.dynamic_slice(tile_mask, (rcv * ROW_TILES, src * COL_TILES), (ROW_TILES, COL_TILES))
    kept = (tiles == 1).T
    rows = jnp.arange(ROW_TILES)[None, :]
    diag_row = jnp.arange(COL_TILES)[:, None] + src * COL_TILES - rcv * ROW_TILES
    diag = rows == diag_row
    plain = (kept & ~diag).astype(jnp.int32)
    count = jnp.sum(plain, axis=1)
    before = jnp.sum(plain[:, None, :] * (rows[0][None, :] < rows[0][:, None]), axis=2)
    hit = (before[:, None, :] == rows[0][None, :, None]) & (plain[:, None, :] == 1)
    order = jnp.sum(jnp.where(hit, rows[0][None, None, :], 0), axis=2)
    diag_on = jnp.sum((kept & diag).astype(jnp.int32), axis=1)
    diag_at = jnp.clip(diag_row[:, 0], 0, ROW_TILES - 1)
    scalars = jnp.stack(
        [jnp.max(kept.astype(jnp.int32))] + [lax.axis_index(name) for name in ("core", "xh", "z", "xl", "y")]
    )
    return jnp.concatenate(
        [count, jnp.zeros((4,), jnp.int32), order.reshape(-1), diag_on, diag_at, scalars]
    ).astype(jnp.int32)


def body(reflection, green, tile_mask, reference_index):
    lines = jnp.transpose(green, (0, 2, 1))
    state = tile_states(tile_mask)
    core = lax.axis_index("core")
    mid = ROWS // 2

    abuf_shape = jax.ShapeDtypeStruct((COL_TILES, 2, ROWS + TILE, TILE), jnp.bfloat16)
    fb_shape = jax.ShapeDtypeStruct((4, P_SIZE, COLS), jnp.bfloat16)
    abuf = pl.pallas_call(
        load_kernel,
        out_shape=abuf_shape,
        in_specs=[smem_spec(), hbm_spec()],
        out_specs=vmem_spec(),
        scratch_shapes=[pltpu.SemaphoreType.DMA((COL_TILES, ROW_TILES + 1))],
        compiler_params=pltpu.CompilerParams(vmem_limit_bytes=12 << 20),
        cost_estimate=pl.CostEstimate(flops=0, transcendentals=0, bytes_accessed=8 << 20),
        name="load",
    )(state, reflection)

    same = lax.dynamic_slice_in_dim(lines, core * mid, mid, 2)
    other = lax.dynamic_slice_in_dim(lines, (1 - core) * mid, mid, 2)
    part_a = lax.ppermute(same, ALL, crossing(0))
    part_b = lax.ppermute(other, ALL, crossing(1))
    beside = lax.ppermute(lines, "xl", SWAP)
    part_a, part_b, beside, abuf = lax.optimization_barrier((part_a, part_b, beside, abuf))

    g_own = jnp.stack([lines, beside])
    own = jnp.stack([part_a, part_b])
    g_after = lax.ppermute(g_own, "y", ring(1))
    g_before = lax.ppermute(g_own, "y", ring(-1))
    after = lax.ppermute(own, "z", ring(1))
    before = lax.ppermute(own, "z", ring(-1))
    near = lax.ppermute(own, "xh", SWAP)
    g_after, g_before, after, before, near = lax.optimization_barrier(
        (g_after, g_before, after, before, near)
    )

    swap = lax.ppermute(jnp.stack([g_own, g_after, g_before]), "core", SWAP)
    g_far_a = lax.ppermute(g_after[0], "y", ring(1))
    g_far_b = lax.ppermute(g_before[1], "y", ring(-1))
    near_after = lax.ppermute(near, "z", ring(1))
    near_before = lax.ppermute(near, "z", ring(-1))
    far_a = lax.ppermute(after, "z", ring(1))
    fb = pl.pallas_call(
        near_kernel,
        out_shape=fb_shape,
        in_specs=[smem_spec()] + [vmem_spec()] * 4,
        out_specs=vmem_spec(),
        scratch_shapes=[pltpu.VMEM((12 * SHARD, 2 * TILE), jnp.float32)],
        compiler_params=pltpu.CompilerParams(vmem_limit_bytes=24 << 20),
        cost_estimate=pl.CostEstimate(flops=3 << 30, transcendentals=0, bytes_accessed=8 << 20),
        name="near",
    )(state, abuf, g_own, g_after, g_before)
    g_far_a, g_far_b, near_after, near_before, fb = lax.optimization_barrier(
        (g_far_a, g_far_b, near_after, near_before, fb)
    )

    swap_far = lax.ppermute(jnp.stack([g_far_a, g_far_b]), "core", SWAP)
    far_b = lax.ppermute(near_before, "z", ring(-1))
    fb = pl.pallas_call(
        swap_kernel,
        out_shape=fb_shape,
        in_specs=[smem_spec()] + [vmem_spec()] * 3,
        out_specs=vmem_spec(),
        scratch_shapes=[pltpu.VMEM((12 * SHARD, 2 * TILE), jnp.float32)],
        input_output_aliases={2: 0},
        compiler_params=pltpu.CompilerParams(vmem_limit_bytes=24 << 20),
        cost_estimate=pl.CostEstimate(flops=3 << 30, transcendentals=0, bytes_accessed=8 << 20),
        name="swap",
    )(state, abuf, fb, swap)

    block = jax.ShapeDtypeStruct((N_CHIPS, 8, P_SIZE), jnp.bfloat16)
    _, keep, send = pl.pallas_call(
        finish_kernel,
        out_shape=(fb_shape, block, block),
        in_specs=[smem_spec()] + [vmem_spec()] * 5 + [any_spec()] * 8,
        out_specs=(vmem_spec(),) * 3,
        scratch_shapes=[
            pltpu.VMEM((2, P_SIZE, COLS), jnp.bfloat16),
            pltpu.VMEM((8 * SHARD, 2 * TILE), jnp.float32),
            pltpu.VMEM((2 * P_SIZE, P_SIZE), jnp.float32),
            pltpu.SemaphoreType.DMA((16,)),
        ],
        input_output_aliases={2: 0},
        compiler_params=pltpu.CompilerParams(vmem_limit_bytes=32 << 20),
        cost_estimate=pl.CostEstimate(flops=6 << 30, transcendentals=0, bytes_accessed=8 << 20),
        name="finish",
    )(
        state, abuf, fb, g_far_a, g_far_b, swap_far,
        own, near, after, before, near_after, near_before, far_a, far_b,
    )
    taken = lax.ppermute(send, "core", SWAP)
    summed = (keep.astype(jnp.float32) + taken.astype(jnp.float32)).astype(jnp.bfloat16)
    parts = lax.all_to_all(summed, CHIPS, 0, 0)
    return pl.pallas_call(
        align_kernel,
        out_shape=jax.ShapeDtypeStruct((4, 2, P_SIZE), jnp.float32),
        in_specs=[smem_spec(), vmem_spec()],
        out_specs=vmem_spec(),
        name="align",
    )(reference_index, parts)


def solution(mesh):
    fine = Mesh(mesh.devices.reshape([size for _, size in PARTS]), [name for name, _ in PARTS])
    return jax.shard_map(
        body,
        mesh=fine,
        in_specs=(P(None, RCV, SRC), P(None, RCV, SRC), P(), P(ALL)),
        out_specs=P(ALL, None, None),
        check_vma=False,
    )
```

```python
import jax
import jax.numpy as jnp
from jax import lax
from jax.experimental import pallas as pl
from jax.experimental.pallas import tpu as pltpu
from jax.sharding import Mesh, PartitionSpec as P

P_SIZE = 512
TILE = 256
PARTS = (("xh", 2), ("z", 4), ("y", 4), ("xl", 2), ("core", 2))
RCV = ("xh", "z")
SRC = ("y", "xl", "core")
ALL = RCV + SRC
CHIPS = RCV + SRC[:2]
ROWS = 2048
COLS = 1024
ROW_TILES = ROWS // TILE
COL_TILES = COLS // TILE
SHARD = 32
N_CHIPS = 64
SWAP = [(0, 1), (1, 0)]


def place(xh, z, y, xl, core):
    return (((xh * 4 + z) * 4 + y) * 2 + xl) * 2 + core


def crossing(cross):
    return [
        (place(xh, z, y, xl, core), place(xl, y, 2 * xh + z // 2, z % 2, core ^ cross))
        for xh in range(2)
        for z in range(4)
        for y in range(4)
        for xl in range(2)
        for core in range(2)
    ]


def ring(step):
    return [(i, (i + step) % 4) for i in range(4)]


def dot(a, b):
    return lax.dot_general(a, b, (((1,), (0,)), ((), ())), preferred_element_type=jnp.float32)


def dot_nt(a, b):
    return lax.dot_general(a, b, (((1,), (1,)), ((), ())), preferred_element_type=jnp.float32)


def load_kernel(st, a, abuf, asem):
    def tile_copy(c, source, i):
        row = pl.multiple_of(source * TILE, TILE)
        return pltpu.make_async_copy(
            a.at[:, pl.ds(row, TILE), pl.ds(c * TILE, TILE)],
            abuf.at[c, :, pl.ds(i * TILE, TILE), :],
            asem.at[c, i],
        )

    def visit(act):
        for c in range(COL_TILES):
            for i in range(ROW_TILES):

                @pl.when(i < st[c])
                def _():
                    act(tile_copy(c, st[8 + c * ROW_TILES + i], i))

            @pl.when(st[40 + c] != 0)
            def _():
                act(tile_copy(c, st[44 + c], ROW_TILES))

    visit(lambda copy: copy.start())
    visit(lambda copy: copy.wait())


def project(st, abuf, acc, fb, left_of, targets):
    def column(c, carry):
        n = st[c]
        lanes = pl.ds(pl.multiple_of(c * TILE, TILE), TILE)

        def product(tiles, start):
            left = jnp.concatenate([left_of(t) for t in tiles], axis=1)
            rows = pl.ds(pl.multiple_of(start * TILE, TILE), len(tiles) * TILE)
            right = jnp.concatenate([abuf[c, 0, rows, :], abuf[c, 1, rows, :]], axis=1)
            return dot(left, right)

        def listed(first, count):
            return [st[8 + c * ROW_TILES + first + i] for i in range(count)]

        @pl.when(n < 4)
        def _():
            acc[...] = jnp.zeros_like(acc)

        @pl.when(n >= 4)
        def _():
            acc[...] = product(listed(0, 4), 0)

        @pl.when(n == 8)
        def _():
            acc[...] += product(listed(4, 4), 4)

        @pl.when((n & 2) != 0)
        def _():
            first = n & 4
            acc[...] += product(listed(first, 2), first)

        @pl.when((n & 1) != 0)
        def _():
            acc[...] += product(listed(n - 1, 1), n - 1)

        def store(front, back):
            for b, row in enumerate(targets):
                rows = pl.ds(pl.multiple_of(row, SHARD), SHARD)
                at = 2 * SHARD * b
                rr = acc[at : at + SHARD, :TILE]
                ri = acc[at : at + SHARD, TILE:]
                ir = acc[at + SHARD : at + 2 * SHARD, :TILE]
                ii = acc[at + SHARD : at + 2 * SHARD, TILE:]
                if front:
                    fb[0, rows, lanes] = (rr + ii).astype(jnp.bfloat16)
                    fb[1, rows, lanes] = (ri - ir).astype(jnp.bfloat16)
                if back:
                    fb[2, rows, lanes] = (rr - ii).astype(jnp.bfloat16)
                    fb[3, rows, lanes] = (ri + ir).astype(jnp.bfloat16)

        @pl.when(st[40 + c] == 0)
        def _():
            store(True, True)

        @pl.when(st[40 + c] != 0)
        def _():
            store(False, True)
            acc[...] += product([st[44 + c]], ROW_TILES)
            store(True, False)

        return carry

    lax.fori_loop(0, COL_TILES, column, 0)


def line_row(st, x_other, y_step, other):
    core, xl, y = st[49], st[52], st[53]
    line = 4 * ((y + y_step + 4) % 4) + 2 * (1 - xl if x_other else xl)
    return (line + (1 - core if other else core)) * SHARD


def tile_lanes(t):
    return pl.ds(pl.multiple_of(t * TILE, TILE), TILE)


def near_kernel(st, abuf, own, after, before, fb, acc):
    @pl.when(st[48] != 0)
    def _():
        def left_of(t):
            return jnp.concatenate(
                [ref[:, :, :, tile_lanes(t)].reshape(4 * SHARD, TILE) for ref in (own, after, before)], axis=0
            )

        targets = [line_row(st, x, step, False) for step in (0, -1, 1) for x in range(2)]
        project(st, abuf, acc, fb, left_of, targets)


def row_copies(st, gbuf, sem, pieces):
    core, xh, z = st[49], st[50], st[51]
    copies = []
    for ref, x_other, z_step in pieces:
        for part in range(2):
            block = 2 * ((z + z_step + 4) % 4) + (1 - xh if x_other else xh)
            slot = core if part == 0 else 1 - core
            row = pl.multiple_of(block * 64 + slot * SHARD, SHARD)
            target = gbuf.at[:, pl.ds(row, SHARD), :]
            copies.append(pltpu.make_async_copy(ref.at[part], target, sem.at[len(copies)]))
    return copies


def rest_kernel(
    st, abuf, fb_in, swap, g_far_a, g_far_b, swap_far,
    own, near, after, before, near_after, near_before,
    fb, gbuf, acc, gsem,
):
    @pl.when(st[48] != 0)
    def _():
        copies = row_copies(
            st,
            gbuf,
            gsem,
            (
                (own, False, 0),
                (near, True, 0),
                (after, False, -1),
                (before, False, 1),
                (near_after, True, -1),
                (near_before, True, 1),
            ),
        )
        for copy in copies:
            copy.start()

        def left_of(t):
            lanes = tile_lanes(t)
            return jnp.concatenate(
                [
                    swap[:, :, :, :, lanes].reshape(12 * SHARD, TILE),
                    g_far_a[:, :, lanes].reshape(2 * SHARD, TILE),
                    g_far_b[:, :, lanes].reshape(2 * SHARD, TILE),
                    swap_far[:, :, :, lanes].reshape(4 * SHARD, TILE),
                ],
                axis=0,
            )

        targets = [line_row(st, x, step, True) for step in (0, -1, 1) for x in range(2)]
        targets += [line_row(st, x, 2, other) for other in (False, True) for x in range(2)]
        project(st, abuf, acc, fb, left_of, targets)
        for copy in copies:
            copy.wait()


def finish_kernel(st, fb, gbuf_in, far_a, far_b, gbuf, keep, send, wide, gsem):
    core = st[49]
    sub = lax.broadcasted_iota(jnp.int32, (N_CHIPS, 8, P_SIZE), 1)
    low = sub < 4

    @pl.when(st[48] != 0)
    def _():
        copies = row_copies(st, gbuf, gsem, ((far_a, False, 2), (far_b, True, 2)))
        for copy in copies:
            copy.start()
        for copy in copies:
            copy.wait()
        for c in range(COL_TILES):
            cols = slice(c * TILE, (c + 1) * TILE)
            gr = gbuf[0, :, cols]
            gi = gbuf[1, :, cols]
            fr = fb[0, :, cols]
            fi = fb[1, :, cols]
            left = jnp.concatenate(
                [
                    jnp.concatenate([fr, -fi, gr, gi], axis=1),
                    jnp.concatenate([fi, fr, -gi, gr], axis=1),
                ],
                axis=0,
            )
            right = jnp.concatenate([gr, gi, fb[2, :, cols], fb[3, :, cols]], axis=1)
            if c == 0:
                wide[...] = dot_nt(left, right)
            else:
                wide[...] += dot_nt(left, right)
        re = wide[:P_SIZE].reshape(N_CHIPS, 8, P_SIZE)
        im = wide[P_SIZE:].reshape(N_CHIPS, 8, P_SIZE)
        first = jnp.where(low, re, pltpu.roll(im, 4, 1)).astype(jnp.bfloat16)
        second = jnp.where(low, pltpu.roll(re, 4, 1), im).astype(jnp.bfloat16)

        @pl.when(core == 0)
        def _():
            keep[...] = first
            send[...] = second

        @pl.when(core != 0)
        def _():
            keep[...] = second
            send[...] = first

    @pl.when(st[48] == 0)
    def _():
        keep[...] = jnp.zeros_like(keep)
        send[...] = jnp.zeros_like(send)


def align_kernel(index, parts, out):
    total = jnp.sum(parts[...].astype(jnp.float32), axis=0)
    lane = lax.broadcasted_iota(jnp.int32, (1, P_SIZE), 1)
    for i in range(4):
        re = total[i : i + 1]
        im = total[4 + i : 5 + i]
        chosen = lane == index[i]
        anchor_re = jnp.sum(jnp.where(chosen, re, 0.0), axis=1, keepdims=True)
        anchor_im = jnp.sum(jnp.where(chosen, im, 0.0), axis=1, keepdims=True)
        out[i, 0:1, :] = re * anchor_re + im * anchor_im
        out[i, 1:2, :] = im * anchor_re - re * anchor_im


def any_spec():
    return pl.BlockSpec(memory_space=pl.ANY)


def hbm_spec():
    return pl.BlockSpec(memory_space=pltpu.HBM)


def smem_spec():
    return pl.BlockSpec(memory_space=pltpu.SMEM)


def vmem_spec():
    return pl.BlockSpec(memory_space=pltpu.VMEM)


def tile_states(tile_mask):
    rcv = lax.axis_index(RCV)
    src = lax.axis_index(SRC)
    tiles = lax.dynamic_slice(tile_mask, (rcv * ROW_TILES, src * COL_TILES), (ROW_TILES, COL_TILES))
    kept = (tiles == 1).T
    rows = jnp.arange(ROW_TILES)[None, :]
    diag_row = jnp.arange(COL_TILES)[:, None] + src * COL_TILES - rcv * ROW_TILES
    diag = rows == diag_row
    plain = (kept & ~diag).astype(jnp.int32)
    count = jnp.sum(plain, axis=1)
    before = jnp.sum(plain[:, None, :] * (rows[0][None, :] < rows[0][:, None]), axis=2)
    hit = (before[:, None, :] == rows[0][None, :, None]) & (plain[:, None, :] == 1)
    order = jnp.sum(jnp.where(hit, rows[0][None, None, :], 0), axis=2)
    diag_on = jnp.sum((kept & diag).astype(jnp.int32), axis=1)
    diag_at = jnp.clip(diag_row[:, 0], 0, ROW_TILES - 1)
    scalars = jnp.stack(
        [jnp.max(kept.astype(jnp.int32))] + [lax.axis_index(name) for name in ("core", "xh", "z", "xl", "y")]
    )
    return jnp.concatenate(
        [count, jnp.zeros((4,), jnp.int32), order.reshape(-1), diag_on, diag_at, scalars]
    ).astype(jnp.int32)


def body(reflection, green, tile_mask, reference_index):
    lines = jnp.transpose(green, (0, 2, 1))
    state = tile_states(tile_mask)
    core = lax.axis_index("core")
    mid = ROWS // 2

    first = lax.optimization_barrier((core, state[48]))[0]
    same = lax.dynamic_slice_in_dim(lines, first * mid, mid, 2)
    other = lax.dynamic_slice_in_dim(lines, (1 - first) * mid, mid, 2)
    part_a = lax.ppermute(same, ALL, crossing(0))
    part_b = lax.ppermute(other, ALL, crossing(1))
    beside = lax.ppermute(lines, "xl", SWAP)

    g_own = jnp.stack([lines, beside])
    own = jnp.stack([part_a, part_b])
    g_after = lax.ppermute(g_own, "y", ring(1))
    g_before = lax.ppermute(g_own, "y", ring(-1))
    after = lax.ppermute(own, "z", ring(1))
    before = lax.ppermute(own, "z", ring(-1))
    near = lax.ppermute(own, "xh", SWAP)
    abuf_shape = jax.ShapeDtypeStruct((COL_TILES, 2, ROWS + TILE, TILE), jnp.bfloat16)
    fb_shape = jax.ShapeDtypeStruct((4, P_SIZE, COLS), jnp.bfloat16)
    abuf = pl.pallas_call(
        load_kernel,
        out_shape=abuf_shape,
        in_specs=[smem_spec(), hbm_spec()],
        out_specs=vmem_spec(),
        scratch_shapes=[pltpu.SemaphoreType.DMA((COL_TILES, ROW_TILES + 1))],
        compiler_params=pltpu.CompilerParams(vmem_limit_bytes=12 << 20),
        cost_estimate=pl.CostEstimate(flops=0, transcendentals=0, bytes_accessed=8 << 20),
        name="load",
    )(state, pltpu.with_memory_space_constraint(reflection, pltpu.HBM))
    g_after, g_before, _ = lax.optimization_barrier((g_after, g_before, own))
    abuf, near, after, before = lax.optimization_barrier((abuf, near, after, before))

    swap = lax.ppermute(jnp.stack([g_own, g_after, g_before]), "core", SWAP)
    g_far_a = lax.ppermute(g_after[0], "y", ring(1))
    g_far_b = lax.ppermute(g_before[1], "y", ring(-1))
    near_after = lax.ppermute(near, "z", ring(1))
    near_before = lax.ppermute(near, "z", ring(-1))
    far_a = lax.ppermute(after, "z", ring(1))
    fb = pl.pallas_call(
        near_kernel,
        out_shape=fb_shape,
        in_specs=[smem_spec()] + [vmem_spec()] * 4,
        out_specs=vmem_spec(),
        scratch_shapes=[pltpu.VMEM((12 * SHARD, 2 * TILE), jnp.float32)],
        compiler_params=pltpu.CompilerParams(vmem_limit_bytes=24 << 20),
        cost_estimate=pl.CostEstimate(flops=3 << 30, transcendentals=0, bytes_accessed=8 << 20),
        name="near",
    )(state, abuf, g_own, g_after, g_before)
    g_far_a, g_far_b, near_after, near_before, fb = lax.optimization_barrier(
        (g_far_a, g_far_b, near_after, near_before, fb)
    )

    swap_far = lax.ppermute(jnp.stack([g_far_a, g_far_b]), "core", SWAP)
    far_b = lax.ppermute(near_before, "z", ring(-1))
    gbuf_shape = jax.ShapeDtypeStruct((2, P_SIZE, COLS), jnp.bfloat16)
    fb, gbuf = pl.pallas_call(
        rest_kernel,
        out_shape=(fb_shape, gbuf_shape),
        in_specs=[smem_spec()] + [vmem_spec()] * 6 + [any_spec()] * 6,
        out_specs=(vmem_spec(), vmem_spec()),
        scratch_shapes=[
            pltpu.VMEM((20 * SHARD, 2 * TILE), jnp.float32),
            pltpu.SemaphoreType.DMA((12,)),
        ],
        input_output_aliases={2: 0},
        compiler_params=pltpu.CompilerParams(vmem_limit_bytes=24 << 20),
        cost_estimate=pl.CostEstimate(flops=5 << 30, transcendentals=0, bytes_accessed=8 << 20),
        name="rest",
    )(
        state, abuf, fb, swap, g_far_a, g_far_b, swap_far,
        own, near, after, before, near_after, near_before,
    )

    block = jax.ShapeDtypeStruct((N_CHIPS, 8, P_SIZE), jnp.bfloat16)
    _, keep, send = pl.pallas_call(
        finish_kernel,
        out_shape=(gbuf_shape, block, block),
        in_specs=[smem_spec(), vmem_spec(), vmem_spec(), any_spec(), any_spec()],
        out_specs=(vmem_spec(),) * 3,
        scratch_shapes=[
            pltpu.VMEM((2 * P_SIZE, P_SIZE), jnp.float32),
            pltpu.SemaphoreType.DMA((4,)),
        ],
        input_output_aliases={2: 0},
        compiler_params=pltpu.CompilerParams(vmem_limit_bytes=32 << 20),
        cost_estimate=pl.CostEstimate(flops=4 << 30, transcendentals=0, bytes_accessed=8 << 20),
        name="finish",
    )(state, fb, gbuf, far_a, far_b)
    taken = lax.ppermute(send, "core", SWAP)
    summed = (keep.astype(jnp.float32) + taken.astype(jnp.float32)).astype(jnp.bfloat16)
    parts = lax.all_to_all(summed, CHIPS, 0, 0)
    return pl.pallas_call(
        align_kernel,
        out_shape=jax.ShapeDtypeStruct((4, 2, P_SIZE), jnp.float32),
        in_specs=[smem_spec(), vmem_spec()],
        out_specs=vmem_spec(),
        name="align",
    )(reference_index, parts)


def solution(mesh):
    fine = Mesh(mesh.devices.reshape([size for _, size in PARTS]), [name for name, _ in PARTS])
    return jax.shard_map(
        body,
        mesh=fine,
        in_specs=(P(None, RCV, SRC), P(None, RCV, SRC), P(), P(ALL)),
        out_specs=P(ALL, None, None),
        check_vma=False,
    )
```

```python
import jax
import jax.numpy as jnp
from jax import lax
from jax.experimental import pallas as pl
from jax.experimental.pallas import tpu as pltpu
from jax.sharding import Mesh, PartitionSpec as P

P_SIZE = 512
TILE = 256
PARTS = (("xh", 2), ("z", 4), ("y", 4), ("xl", 2), ("core", 2))
RCV = ("xh", "z")
SRC = ("y", "xl", "core")
ALL = RCV + SRC
CHIPS = RCV + SRC[:2]
ROWS = 2048
COLS = 1024
ROW_TILES = ROWS // TILE
COL_TILES = COLS // TILE
SHARD = 32
N_CHIPS = 64
SWAP = [(0, 1), (1, 0)]


def place(xh, z, y, xl, core):
    return (((xh * 4 + z) * 4 + y) * 2 + xl) * 2 + core


def crossing(cross):
    return [
        (place(xh, z, y, xl, core), place(xl, y, 2 * xh + z // 2, z % 2, core ^ cross))
        for xh in range(2)
        for z in range(4)
        for y in range(4)
        for xl in range(2)
        for core in range(2)
    ]


def ring(step):
    return [(i, (i + step) % 4) for i in range(4)]


def dot(a, b):
    return lax.dot_general(a, b, (((1,), (0,)), ((), ())), preferred_element_type=jnp.float32)


def dot_nt(a, b):
    return lax.dot_general(a, b, (((1,), (1,)), ((), ())), preferred_element_type=jnp.float32)


def load_kernel(st, a, abuf, asem):
    def tile_copy(c, source, i):
        row = pl.multiple_of(source * TILE, TILE)
        return pltpu.make_async_copy(
            a.at[:, pl.ds(row, TILE), pl.ds(c * TILE, TILE)],
            abuf.at[c, :, pl.ds(i * TILE, TILE), :],
            asem.at[c, i],
        )

    def visit(act):
        for c in range(COL_TILES):
            for i in range(ROW_TILES):

                @pl.when(i < st[c])
                def _():
                    act(tile_copy(c, st[8 + c * ROW_TILES + i], i))

            @pl.when(st[40 + c] != 0)
            def _():
                act(tile_copy(c, st[44 + c], ROW_TILES))

    visit(lambda copy: copy.start())
    visit(lambda copy: copy.wait())


BLOCK = 2 * SHARD


def accumulators(blocks):
    return [pltpu.ACC(unit)((BLOCK, TILE), jnp.float32) for unit in range(2) for _ in range(blocks)]


def project(st, abuf, accs, saved, fb, left_of, targets):
    blocks = len(targets)

    def push(c, i):
        rows = pl.ds(pl.multiple_of(i * TILE, TILE), TILE)
        for unit in range(2):
            pltpu.matmul_push_rhs(abuf[c, unit, rows, :], 0, unit)

    def stream(t, after_first=None):
        left = left_of(t)
        for b in range(blocks):
            for unit in range(2):
                pltpu.matmul_acc_lhs(
                    accs[unit * blocks + b],
                    left[b * BLOCK : (b + 1) * BLOCK],
                    load_staged_rhs=0 if b == 0 else None,
                )
            if b == 0 and after_first:
                after_first()

    def column(c, carry):
        n = st[c]
        on_diag = st[40 + c] != 0
        lanes = pl.ds(pl.multiple_of(c * TILE, TILE), TILE)

        def popped(b):
            by_real = pltpu.matmul_pop(accs[b])
            by_imag = pltpu.matmul_pop(accs[blocks + b])
            return by_real[:SHARD], by_imag[:SHARD], by_real[SHARD:], by_imag[SHARD:]

        @pl.when(n > 0)
        def _():
            push(c, 0)

            def step(i, inner):
                stream(st[8 + c * ROW_TILES + i], lambda: push(c, i + 1))
                return inner

            lax.fori_loop(0, n - 1, step, 0)
            stream(st[8 + c * ROW_TILES + n - 1])

        for b, row in enumerate(targets):
            rows = pl.ds(pl.multiple_of(row, SHARD), SHARD)
            rr, ri, ir, ii = popped(b)
            fb[0, rows, lanes] = (rr + ii).astype(jnp.bfloat16)
            fb[1, rows, lanes] = (ri - ir).astype(jnp.bfloat16)
            fb[2, rows, lanes] = (rr - ii).astype(jnp.bfloat16)
            fb[3, rows, lanes] = (ri + ir).astype(jnp.bfloat16)

            @pl.when(on_diag)
            def _():
                saved[0, b * SHARD : (b + 1) * SHARD, :] = rr + ii
                saved[1, b * SHARD : (b + 1) * SHARD, :] = ri - ir

        @pl.when(on_diag)
        def _():
            push(c, ROW_TILES)
            stream(st[44 + c])
            for b, row in enumerate(targets):
                rows = pl.ds(pl.multiple_of(row, SHARD), SHARD)
                rr, ri, ir, ii = popped(b)
                at = slice(b * SHARD, (b + 1) * SHARD)
                fb[0, rows, lanes] = (saved[0, at, :] + (rr + ii)).astype(jnp.bfloat16)
                fb[1, rows, lanes] = (saved[1, at, :] + (ri - ir)).astype(jnp.bfloat16)

        return carry

    lax.fori_loop(0, COL_TILES, column, 0)


def line_row(st, x_other, y_step, other):
    core, xl, y = st[49], st[52], st[53]
    line = 4 * ((y + y_step + 4) % 4) + 2 * (1 - xl if x_other else xl)
    return (line + (1 - core if other else core)) * SHARD


def tile_lanes(t):
    return pl.ds(pl.multiple_of(t * TILE, TILE), TILE)


def near_kernel(st, abuf, own, after, before, fb, saved):
    @pl.when(st[48] != 0)
    def _():
        def left_of(t):
            return jnp.concatenate(
                [ref[:, :, :, tile_lanes(t)].reshape(4 * SHARD, TILE) for ref in (own, after, before)], axis=0
            )

        targets = [line_row(st, x, step, False) for step in (0, -1, 1) for x in range(2)]
        pl.run_scoped(
            lambda *accs: project(st, abuf, accs, saved, fb, left_of, targets), *accumulators(len(targets))
        )


def row_copies(st, gbuf, sem, pieces):
    core, xh, z = st[49], st[50], st[51]
    copies = []
    for ref, x_other, z_step in pieces:
        for part in range(2):
            block = 2 * ((z + z_step + 4) % 4) + (1 - xh if x_other else xh)
            slot = core if part == 0 else 1 - core
            row = pl.multiple_of(block * 64 + slot * SHARD, SHARD)
            target = gbuf.at[:, pl.ds(row, SHARD), :]
            copies.append(pltpu.make_async_copy(ref.at[part], target, sem.at[len(copies)]))
    return copies


def rest_kernel(
    st, abuf, fb_in, swap, g_far_a, g_far_b, swap_far,
    own, near, after, before, near_after, near_before,
    fb, gbuf, saved, gsem,
):
    @pl.when(st[48] != 0)
    def _():
        copies = row_copies(
            st,
            gbuf,
            gsem,
            (
                (own, False, 0),
                (near, True, 0),
                (after, False, -1),
                (before, False, 1),
                (near_after, True, -1),
                (near_before, True, 1),
            ),
        )
        for copy in copies:
            copy.start()

        def left_of(t):
            lanes = tile_lanes(t)
            return jnp.concatenate(
                [
                    swap[:, :, :, :, lanes].reshape(12 * SHARD, TILE),
                    g_far_a[:, :, lanes].reshape(2 * SHARD, TILE),
                    g_far_b[:, :, lanes].reshape(2 * SHARD, TILE),
                    swap_far[:, :, :, lanes].reshape(4 * SHARD, TILE),
                ],
                axis=0,
            )

        targets = [line_row(st, x, step, True) for step in (0, -1, 1) for x in range(2)]
        targets += [line_row(st, x, 2, other) for other in (False, True) for x in range(2)]
        pl.run_scoped(
            lambda *accs: project(st, abuf, accs, saved, fb, left_of, targets), *accumulators(len(targets))
        )
        for copy in copies:
            copy.wait()


def finish_kernel(st, fb, gbuf_in, far_a, far_b, gbuf, keep, send, gsem):
    core = st[49]
    half = P_SIZE
    blocks = 2 * half // BLOCK
    chips = BLOCK // 8
    low = lax.broadcasted_iota(jnp.int32, (chips, 8, TILE), 1) < 4

    @pl.when(st[48] != 0)
    def _():
        copies = row_copies(st, gbuf, gsem, ((far_a, False, 2), (far_b, True, 2)))
        for copy in copies:
            copy.start()
        for copy in copies:
            copy.wait()

        steps = []
        for c in range(COL_TILES):
            cols = slice(c * TILE, (c + 1) * TILE)
            steps += [
                (lambda cols=cols: (fb[0, :, cols], fb[1, :, cols]), (gbuf, 0, cols)),
                (lambda cols=cols: (-fb[1, :, cols], fb[0, :, cols]), (gbuf, 1, cols)),
                (lambda cols=cols: (gbuf[0, :, cols], -gbuf[1, :, cols]), (fb, 2, cols)),
                (lambda cols=cols: (gbuf[1, :, cols], gbuf[0, :, cols]), (fb, 3, cols)),
            ]

        def push(step):
            ref, slot, cols = steps[step][1]
            for unit in range(2):
                right = ref[slot, unit * TILE : (unit + 1) * TILE, cols]
                pltpu.matmul_push_rhs(right, 0, unit, transpose=True)

        def multiply(*accs):
            push(0)
            for step in range(len(steps)):
                top, bottom = steps[step][0]()
                for b in range(blocks):
                    source = top if b < blocks // 2 else bottom
                    at = (b % (blocks // 2)) * BLOCK
                    for unit in range(2):
                        pltpu.matmul_acc_lhs(
                            accs[unit * blocks + b],
                            source[at : at + BLOCK],
                            load_staged_rhs=0 if b == 0 else None,
                        )
                    if b == 0 and step + 1 < len(steps):
                        push(step + 1)

            for b in range(blocks // 2):
                for unit in range(2):
                    re = pltpu.matmul_pop(accs[unit * blocks + b]).reshape(chips, 8, TILE)
                    im = pltpu.matmul_pop(accs[unit * blocks + blocks // 2 + b]).reshape(chips, 8, TILE)
                    first = jnp.where(low, re, pltpu.roll(im, 4, 1)).astype(jnp.bfloat16)
                    second = jnp.where(low, pltpu.roll(re, 4, 1), im).astype(jnp.bfloat16)
                    at = slice(b * chips, (b + 1) * chips)
                    lanes = slice(unit * TILE, (unit + 1) * TILE)

                    @pl.when(core == 0)
                    def _():
                        keep[at, :, lanes] = first
                        send[at, :, lanes] = second

                    @pl.when(core != 0)
                    def _():
                        keep[at, :, lanes] = second
                        send[at, :, lanes] = first

        pl.run_scoped(multiply, *accumulators(blocks))

    @pl.when(st[48] == 0)
    def _():
        keep[...] = jnp.zeros_like(keep)
        send[...] = jnp.zeros_like(send)


def align_kernel(index, parts, out):
    total = jnp.sum(parts[...].astype(jnp.float32), axis=0)
    lane = lax.broadcasted_iota(jnp.int32, (1, P_SIZE), 1)
    for i in range(4):
        re = total[i : i + 1]
        im = total[4 + i : 5 + i]
        chosen = lane == index[i]
        anchor_re = jnp.sum(jnp.where(chosen, re, 0.0), axis=1, keepdims=True)
        anchor_im = jnp.sum(jnp.where(chosen, im, 0.0), axis=1, keepdims=True)
        out[i, 0:1, :] = re * anchor_re + im * anchor_im
        out[i, 1:2, :] = im * anchor_re - re * anchor_im


def any_spec():
    return pl.BlockSpec(memory_space=pl.ANY)


def hbm_spec():
    return pl.BlockSpec(memory_space=pltpu.HBM)


def smem_spec():
    return pl.BlockSpec(memory_space=pltpu.SMEM)


def vmem_spec():
    return pl.BlockSpec(memory_space=pltpu.VMEM)


def tile_states(tile_mask):
    rcv = lax.axis_index(RCV)
    src = lax.axis_index(SRC)
    tiles = lax.dynamic_slice(tile_mask, (rcv * ROW_TILES, src * COL_TILES), (ROW_TILES, COL_TILES))
    kept = (tiles == 1).T
    rows = jnp.arange(ROW_TILES)[None, :]
    diag_row = jnp.arange(COL_TILES)[:, None] + src * COL_TILES - rcv * ROW_TILES
    diag = rows == diag_row
    plain = (kept & ~diag).astype(jnp.int32)
    count = jnp.sum(plain, axis=1)
    before = jnp.sum(plain[:, None, :] * (rows[0][None, :] < rows[0][:, None]), axis=2)
    hit = (before[:, None, :] == rows[0][None, :, None]) & (plain[:, None, :] == 1)
    order = jnp.sum(jnp.where(hit, rows[0][None, None, :], 0), axis=2)
    diag_on = jnp.sum((kept & diag).astype(jnp.int32), axis=1)
    diag_at = jnp.clip(diag_row[:, 0], 0, ROW_TILES - 1)
    scalars = jnp.stack(
        [jnp.max(kept.astype(jnp.int32))] + [lax.axis_index(name) for name in ("core", "xh", "z", "xl", "y")]
    )
    return jnp.concatenate(
        [count, jnp.zeros((4,), jnp.int32), order.reshape(-1), diag_on, diag_at, scalars]
    ).astype(jnp.int32)


def body(reflection, green, tile_mask, reference_index):
    lines = jnp.transpose(green, (0, 2, 1))
    state = tile_states(tile_mask)
    core = lax.axis_index("core")
    mid = ROWS // 2

    first = lax.optimization_barrier((core, state[48]))[0]
    same = lax.dynamic_slice_in_dim(lines, first * mid, mid, 2)
    other = lax.dynamic_slice_in_dim(lines, (1 - first) * mid, mid, 2)
    part_a = lax.ppermute(same, ALL, crossing(0))
    part_b = lax.ppermute(other, ALL, crossing(1))
    beside = lax.ppermute(lines, "xl", SWAP)

    g_own = jnp.stack([lines, beside])
    own = jnp.stack([part_a, part_b])
    g_after = lax.ppermute(g_own, "y", ring(1))
    g_before = lax.ppermute(g_own, "y", ring(-1))
    after = lax.ppermute(own, "z", ring(1))
    before = lax.ppermute(own, "z", ring(-1))
    near = lax.ppermute(own, "xh", SWAP)
    abuf_shape = jax.ShapeDtypeStruct((COL_TILES, 2, ROWS + TILE, TILE), jnp.bfloat16)
    fb_shape = jax.ShapeDtypeStruct((4, P_SIZE, COLS), jnp.bfloat16)
    abuf = pl.pallas_call(
        load_kernel,
        out_shape=abuf_shape,
        in_specs=[smem_spec(), hbm_spec()],
        out_specs=vmem_spec(),
        scratch_shapes=[pltpu.SemaphoreType.DMA((COL_TILES, ROW_TILES + 1))],
        compiler_params=pltpu.CompilerParams(vmem_limit_bytes=12 << 20),
        cost_estimate=pl.CostEstimate(flops=0, transcendentals=0, bytes_accessed=8 << 20),
        name="load",
    )(state, pltpu.with_memory_space_constraint(reflection, pltpu.HBM))
    g_after, g_before, _ = lax.optimization_barrier((g_after, g_before, own))
    abuf, near, after, before = lax.optimization_barrier((abuf, near, after, before))

    swap = lax.ppermute(jnp.stack([g_own, g_after, g_before]), "core", SWAP)
    g_far_a = lax.ppermute(g_after[0], "y", ring(1))
    g_far_b = lax.ppermute(g_before[1], "y", ring(-1))
    near_after = lax.ppermute(near, "z", ring(1))
    near_before = lax.ppermute(near, "z", ring(-1))
    far_a = lax.ppermute(after, "z", ring(1))
    fb = pl.pallas_call(
        near_kernel,
        out_shape=fb_shape,
        in_specs=[smem_spec()] + [vmem_spec()] * 4,
        out_specs=vmem_spec(),
        scratch_shapes=[pltpu.VMEM((2, 6 * SHARD, TILE), jnp.float32)],
        compiler_params=pltpu.CompilerParams(vmem_limit_bytes=24 << 20),
        cost_estimate=pl.CostEstimate(flops=3 << 30, transcendentals=0, bytes_accessed=8 << 20),
        name="near",
    )(state, abuf, g_own, g_after, g_before)
    g_far_a, g_far_b, near_after, near_before, fb = lax.optimization_barrier(
        (g_far_a, g_far_b, near_after, near_before, fb)
    )

    swap_far = lax.ppermute(jnp.stack([g_far_a, g_far_b]), "core", SWAP)
    far_b = lax.ppermute(near_before, "z", ring(-1))
    gbuf_shape = jax.ShapeDtypeStruct((2, P_SIZE, COLS), jnp.bfloat16)
    fb, gbuf = pl.pallas_call(
        rest_kernel,
        out_shape=(fb_shape, gbuf_shape),
        in_specs=[smem_spec()] + [vmem_spec()] * 6 + [any_spec()] * 6,
        out_specs=(vmem_spec(), vmem_spec()),
        scratch_shapes=[
            pltpu.VMEM((2, 10 * SHARD, TILE), jnp.float32),
            pltpu.SemaphoreType.DMA((12,)),
        ],
        input_output_aliases={2: 0},
        compiler_params=pltpu.CompilerParams(vmem_limit_bytes=24 << 20),
        cost_estimate=pl.CostEstimate(flops=5 << 30, transcendentals=0, bytes_accessed=8 << 20),
        name="rest",
    )(
        state, abuf, fb, swap, g_far_a, g_far_b, swap_far,
        own, near, after, before, near_after, near_before,
    )

    block = jax.ShapeDtypeStruct((N_CHIPS, 8, P_SIZE), jnp.bfloat16)
    _, keep, send = pl.pallas_call(
        finish_kernel,
        out_shape=(gbuf_shape, block, block),
        in_specs=[smem_spec(), vmem_spec(), vmem_spec(), any_spec(), any_spec()],
        out_specs=(vmem_spec(),) * 3,
        scratch_shapes=[pltpu.SemaphoreType.DMA((4,))],
        input_output_aliases={2: 0},
        compiler_params=pltpu.CompilerParams(vmem_limit_bytes=32 << 20),
        cost_estimate=pl.CostEstimate(flops=4 << 30, transcendentals=0, bytes_accessed=8 << 20),
        name="finish",
    )(state, fb, gbuf, far_a, far_b)
    taken = lax.ppermute(send, "core", SWAP)
    summed = (keep.astype(jnp.float32) + taken.astype(jnp.float32)).astype(jnp.bfloat16)
    parts = lax.all_to_all(summed, CHIPS, 0, 0)
    return pl.pallas_call(
        align_kernel,
        out_shape=jax.ShapeDtypeStruct((4, 2, P_SIZE), jnp.float32),
        in_specs=[smem_spec(), vmem_spec()],
        out_specs=vmem_spec(),
        name="align",
    )(reference_index, parts)


def solution(mesh):
    fine = Mesh(mesh.devices.reshape([size for _, size in PARTS]), [name for name, _ in PARTS])
    return jax.shard_map(
        body,
        mesh=fine,
        in_specs=(P(None, RCV, SRC), P(None, RCV, SRC), P(), P(ALL)),
        out_specs=P(ALL, None, None),
        check_vma=False,
    )
```

```python
import jax
import jax.numpy as jnp
from jax import lax
from jax.experimental import pallas as pl
from jax.experimental.pallas import tpu as pltpu
from jax.sharding import Mesh, PartitionSpec as P

P_SIZE = 512
TILE = 256
PARTS = (("xh", 2), ("z", 4), ("y", 4), ("xl", 2), ("core", 2))
RCV = ("xh", "z")
SRC = ("y", "xl", "core")
ALL = RCV + SRC
CHIPS = RCV + SRC[:2]
ROWS = 2048
COLS = 1024
ROW_TILES = ROWS // TILE
COL_TILES = COLS // TILE
SHARD = 32
N_CHIPS = 64
SWAP = [(0, 1), (1, 0)]


def place(xh, z, y, xl, core):
    return (((xh * 4 + z) * 4 + y) * 2 + xl) * 2 + core


def crossing(cross):
    return [
        (place(xh, z, y, xl, core), place(xl, y, 2 * xh + z // 2, z % 2, core ^ cross))
        for xh in range(2)
        for z in range(4)
        for y in range(4)
        for xl in range(2)
        for core in range(2)
    ]


def ring(step):
    return [(i, (i + step) % 4) for i in range(4)]


def dot(a, b):
    return lax.dot_general(a, b, (((1,), (0,)), ((), ())), preferred_element_type=jnp.float32)


def dot_nt(a, b):
    return lax.dot_general(a, b, (((1,), (1,)), ((), ())), preferred_element_type=jnp.float32)


def load_kernel(st, a, abuf, asem):
    def tile_copy(c, source, i):
        row = pl.multiple_of(source * TILE, TILE)
        return pltpu.make_async_copy(
            a.at[:, pl.ds(row, TILE), pl.ds(c * TILE, TILE)],
            abuf.at[c, :, pl.ds(i * TILE, TILE), :],
            asem.at[c, i],
        )

    def visit(act):
        for c in range(COL_TILES):
            for i in range(ROW_TILES):

                @pl.when(i < st[c])
                def _():
                    act(tile_copy(c, st[8 + c * ROW_TILES + i], i))

            @pl.when(st[40 + c] != 0)
            def _():
                act(tile_copy(c, st[44 + c], ROW_TILES))

    visit(lambda copy: copy.start())
    visit(lambda copy: copy.wait())


BLOCK = 2 * SHARD


def accumulators(blocks):
    return [pltpu.ACC(unit)((BLOCK, TILE), jnp.float32) for unit in range(2) for _ in range(blocks)]


def project(st, abuf, accs, saved, fb, left_of, targets):
    blocks = len(targets)

    def push(c, i):
        rows = pl.ds(pl.multiple_of(i * TILE, TILE), TILE)
        for unit in range(2):
            pltpu.matmul_push_rhs(abuf[c, unit, rows, :], 0, unit)

    def stream(t, after_first=None):
        left = left_of(t)
        for b in range(blocks):
            for unit in range(2):
                pltpu.matmul_acc_lhs(
                    accs[unit * blocks + b],
                    left[b * BLOCK : (b + 1) * BLOCK],
                    load_staged_rhs=0 if b == 0 else None,
                )
            if b == 0 and after_first:
                after_first()

    def column(c, carry):
        n = st[c]
        on_diag = st[40 + c] != 0
        lanes = pl.ds(pl.multiple_of(c * TILE, TILE), TILE)

        def popped(b):
            by_real = pltpu.matmul_pop(accs[b])
            by_imag = pltpu.matmul_pop(accs[blocks + b])
            return by_real[:SHARD], by_imag[:SHARD], by_real[SHARD:], by_imag[SHARD:]

        @pl.when(n > 0)
        def _():
            push(c, 0)

            def step(i, inner):
                stream(st[8 + c * ROW_TILES + i], lambda: push(c, i + 1))
                return inner

            lax.fori_loop(0, n - 1, step, 0)
            stream(st[8 + c * ROW_TILES + n - 1])

        def flush(save):
            for b, row in enumerate(targets):
                rows = pl.ds(pl.multiple_of(row, SHARD), SHARD)
                rr, ri, ir, ii = popped(b)
                fb[2, rows, lanes] = (rr - ii).astype(jnp.bfloat16)
                fb[3, rows, lanes] = (ri + ir).astype(jnp.bfloat16)
                if save:
                    saved[0, b * SHARD : (b + 1) * SHARD, :] = rr + ii
                    saved[1, b * SHARD : (b + 1) * SHARD, :] = ri - ir
                else:
                    fb[0, rows, lanes] = (rr + ii).astype(jnp.bfloat16)
                    fb[1, rows, lanes] = (ri - ir).astype(jnp.bfloat16)

        @pl.when(jnp.logical_not(on_diag))
        def _():
            flush(False)

        @pl.when(on_diag)
        def _():
            flush(True)
            push(c, ROW_TILES)
            stream(st[44 + c])
            for b, row in enumerate(targets):
                rows = pl.ds(pl.multiple_of(row, SHARD), SHARD)
                rr, ri, ir, ii = popped(b)
                at = slice(b * SHARD, (b + 1) * SHARD)
                fb[0, rows, lanes] = (saved[0, at, :] + (rr + ii)).astype(jnp.bfloat16)
                fb[1, rows, lanes] = (saved[1, at, :] + (ri - ir)).astype(jnp.bfloat16)

        return carry

    lax.fori_loop(0, COL_TILES, column, 0)


def line_row(st, x_other, y_step, other):
    core, xl, y = st[49], st[52], st[53]
    line = 4 * ((y + y_step + 4) % 4) + 2 * (1 - xl if x_other else xl)
    return (line + (1 - core if other else core)) * SHARD


def tile_lanes(t):
    return pl.ds(pl.multiple_of(t * TILE, TILE), TILE)


def near_kernel(st, abuf, own, after, before, fb, saved):
    @pl.when(st[48] != 0)
    def _():
        def left_of(t):
            return jnp.concatenate(
                [ref[:, :, :, tile_lanes(t)].reshape(4 * SHARD, TILE) for ref in (own, after, before)], axis=0
            )

        targets = [line_row(st, x, step, False) for step in (0, -1, 1) for x in range(2)]
        pl.run_scoped(
            lambda *accs: project(st, abuf, accs, saved, fb, left_of, targets), *accumulators(len(targets))
        )


def row_copies(st, gbuf, sem, pieces):
    core, xh, z = st[49], st[50], st[51]
    copies = []
    for ref, x_other, z_step in pieces:
        for part in range(2):
            block = 2 * ((z + z_step + 4) % 4) + (1 - xh if x_other else xh)
            slot = core if part == 0 else 1 - core
            row = pl.multiple_of(block * 64 + slot * SHARD, SHARD)
            target = gbuf.at[:, pl.ds(row, SHARD), :]
            copies.append(pltpu.make_async_copy(ref.at[part], target, sem.at[len(copies)]))
    return copies


def rest_kernel(
    st, abuf, fb_in, swap, g_far_a, g_far_b, swap_far_a, swap_far_b,
    own, near, after, before, near_after, near_before,
    fb, gbuf, saved, gsem,
):
    @pl.when(st[48] != 0)
    def _():
        copies = row_copies(
            st,
            gbuf,
            gsem,
            (
                (own, False, 0),
                (near, True, 0),
                (after, False, -1),
                (before, False, 1),
                (near_after, True, -1),
                (near_before, True, 1),
            ),
        )
        for copy in copies:
            copy.start()

        def left_of(t):
            lanes = tile_lanes(t)
            return jnp.concatenate(
                [
                    swap[:, :, :, :, lanes].reshape(12 * SHARD, TILE),
                ]
                + [
                    ref[:, :, lanes].reshape(2 * SHARD, TILE)
                    for ref in (g_far_a, g_far_b, swap_far_a, swap_far_b)
                ],
                axis=0,
            )

        targets = [line_row(st, x, step, True) for step in (0, -1, 1) for x in range(2)]
        targets += [line_row(st, x, 2, other) for other in (False, True) for x in range(2)]
        pl.run_scoped(
            lambda *accs: project(st, abuf, accs, saved, fb, left_of, targets), *accumulators(len(targets))
        )
        for copy in copies:
            copy.wait()


def finish_kernel(st, fb, gbuf_in, far_a, far_b, gbuf, keep, send, gsem):
    core = st[49]
    half = P_SIZE
    blocks = 2 * half // BLOCK
    chips = BLOCK // 8
    low = lax.broadcasted_iota(jnp.int32, (chips, 8, TILE), 1) < 4

    @pl.when(st[48] != 0)
    def _():
        copies = row_copies(st, gbuf, gsem, ((far_a, False, 2), (far_b, True, 2)))
        for copy in copies:
            copy.start()
        for copy in copies:
            copy.wait()

        steps = []
        for c in range(COL_TILES):
            cols = slice(c * TILE, (c + 1) * TILE)
            steps += [
                (lambda cols=cols: (fb[0, :, cols], fb[1, :, cols]), (gbuf, 0, cols)),
                (lambda cols=cols: (-fb[1, :, cols], fb[0, :, cols]), (gbuf, 1, cols)),
                (lambda cols=cols: (gbuf[0, :, cols], -gbuf[1, :, cols]), (fb, 2, cols)),
                (lambda cols=cols: (gbuf[1, :, cols], gbuf[0, :, cols]), (fb, 3, cols)),
            ]

        def push(step):
            ref, slot, cols = steps[step][1]
            for unit in range(2):
                right = ref[slot, unit * TILE : (unit + 1) * TILE, cols]
                pltpu.matmul_push_rhs(right, 0, unit, transpose=True)

        def multiply(*accs):
            push(0)
            for step in range(len(steps)):
                top, bottom = steps[step][0]()
                for b in range(blocks):
                    source = top if b < blocks // 2 else bottom
                    at = (b % (blocks // 2)) * BLOCK
                    for unit in range(2):
                        pltpu.matmul_acc_lhs(
                            accs[unit * blocks + b],
                            source[at : at + BLOCK],
                            load_staged_rhs=0 if b == 0 else None,
                        )
                    if b == 0 and step + 1 < len(steps):
                        push(step + 1)

            for b in range(blocks // 2):
                for unit in range(2):
                    re = pltpu.matmul_pop(accs[unit * blocks + b]).reshape(chips, 8, TILE)
                    im = pltpu.matmul_pop(accs[unit * blocks + blocks // 2 + b]).reshape(chips, 8, TILE)
                    first = jnp.where(low, re, pltpu.roll(im, 4, 1))
                    second = jnp.where(low, pltpu.roll(re, 4, 1), im)
                    at = slice(b * chips, (b + 1) * chips)
                    lanes = slice(unit * TILE, (unit + 1) * TILE)

                    keep[at, :, lanes] = jnp.where(core == 0, first, second).astype(jnp.bfloat16)
                    send[at, :, lanes] = jnp.where(core == 0, second, first).astype(jnp.bfloat16)

        pl.run_scoped(multiply, *accumulators(blocks))

    @pl.when(st[48] == 0)
    def _():
        keep[...] = jnp.zeros_like(keep)
        send[...] = jnp.zeros_like(send)


def align_kernel(index, parts, out):
    total = jnp.sum(parts[...].astype(jnp.float32), axis=0)
    lane = lax.broadcasted_iota(jnp.int32, (1, P_SIZE), 1)
    for i in range(4):
        re = total[i : i + 1]
        im = total[4 + i : 5 + i]
        chosen = lane == index[i]
        anchor_re = jnp.sum(jnp.where(chosen, re, 0.0), axis=1, keepdims=True)
        anchor_im = jnp.sum(jnp.where(chosen, im, 0.0), axis=1, keepdims=True)
        out[i, 0:1, :] = re * anchor_re + im * anchor_im
        out[i, 1:2, :] = im * anchor_re - re * anchor_im


def any_spec():
    return pl.BlockSpec(memory_space=pl.ANY)


def hbm_spec():
    return pl.BlockSpec(memory_space=pltpu.HBM)


def smem_spec():
    return pl.BlockSpec(memory_space=pltpu.SMEM)


def vmem_spec():
    return pl.BlockSpec(memory_space=pltpu.VMEM)


def tile_states(tile_mask):
    rcv = lax.axis_index(RCV)
    src = lax.axis_index(SRC)
    tiles = lax.dynamic_slice(tile_mask, (rcv * ROW_TILES, src * COL_TILES), (ROW_TILES, COL_TILES))
    kept = (tiles == 1).T
    rows = jnp.arange(ROW_TILES)[None, :]
    diag_row = jnp.arange(COL_TILES)[:, None] + src * COL_TILES - rcv * ROW_TILES
    diag = rows == diag_row
    plain = (kept & ~diag).astype(jnp.int32)
    count = jnp.sum(plain, axis=1)
    before = jnp.sum(plain[:, None, :] * (rows[0][None, :] < rows[0][:, None]), axis=2)
    hit = (before[:, None, :] == rows[0][None, :, None]) & (plain[:, None, :] == 1)
    order = jnp.sum(jnp.where(hit, rows[0][None, None, :], 0), axis=2)
    diag_on = jnp.sum((kept & diag).astype(jnp.int32), axis=1)
    diag_at = jnp.clip(diag_row[:, 0], 0, ROW_TILES - 1)
    scalars = jnp.stack(
        [jnp.max(kept.astype(jnp.int32))] + [lax.axis_index(name) for name in ("core", "xh", "z", "xl", "y")]
    )
    return jnp.concatenate(
        [count, jnp.zeros((4,), jnp.int32), order.reshape(-1), diag_on, diag_at, scalars]
    ).astype(jnp.int32)


def body(reflection, green, tile_mask, reference_index):
    lines = jnp.transpose(green, (0, 2, 1))
    state = tile_states(tile_mask)
    core = lax.axis_index("core")
    mid = ROWS // 2

    first = lax.optimization_barrier((core, state[48]))[0]
    same = lax.dynamic_slice_in_dim(lines, first * mid, mid, 2)
    other = lax.dynamic_slice_in_dim(lines, (1 - first) * mid, mid, 2)
    part_a = lax.ppermute(same, ALL, crossing(0))
    part_b = lax.ppermute(other, ALL, crossing(1))
    beside = lax.ppermute(lines, "xl", SWAP)

    g_own = jnp.stack([lines, beside])
    own = jnp.stack([part_a, part_b])
    g_after = lax.ppermute(g_own, "y", ring(1))
    g_before = lax.ppermute(g_own, "y", ring(-1))
    after = lax.ppermute(own, "z", ring(1))
    before = lax.ppermute(own, "z", ring(-1))
    near = lax.ppermute(own, "xh", SWAP)
    abuf_shape = jax.ShapeDtypeStruct((COL_TILES, 2, ROWS + TILE, TILE), jnp.bfloat16)
    fb_shape = jax.ShapeDtypeStruct((4, P_SIZE, COLS), jnp.bfloat16)
    abuf = pl.pallas_call(
        load_kernel,
        out_shape=abuf_shape,
        in_specs=[smem_spec(), hbm_spec()],
        out_specs=vmem_spec(),
        scratch_shapes=[pltpu.SemaphoreType.DMA((COL_TILES, ROW_TILES + 1))],
        compiler_params=pltpu.CompilerParams(vmem_limit_bytes=12 << 20),
        cost_estimate=pl.CostEstimate(flops=0, transcendentals=0, bytes_accessed=8 << 20),
        name="load",
    )(state, pltpu.with_memory_space_constraint(reflection, pltpu.HBM))
    abuf, near, after, before = lax.optimization_barrier((abuf, near, after, before))
    g_after, g_before, _, _ = lax.optimization_barrier((g_after, g_before, near, abuf))

    swap = lax.ppermute(jnp.stack([g_own, g_after, g_before]), "core", SWAP)
    g_far_a = lax.ppermute(g_after[0], "y", ring(1))
    g_far_b = lax.ppermute(g_before[1], "y", ring(-1))
    near_after = lax.ppermute(near, "z", ring(1))
    near_before = lax.ppermute(near, "z", ring(-1))
    far_a = lax.ppermute(after, "z", ring(1))
    fb = pl.pallas_call(
        near_kernel,
        out_shape=fb_shape,
        in_specs=[smem_spec()] + [vmem_spec()] * 4,
        out_specs=vmem_spec(),
        scratch_shapes=[pltpu.VMEM((2, 6 * SHARD, TILE), jnp.float32)],
        compiler_params=pltpu.CompilerParams(vmem_limit_bytes=24 << 20),
        cost_estimate=pl.CostEstimate(flops=3 << 30, transcendentals=0, bytes_accessed=8 << 20),
        name="near",
    )(state, abuf, g_own, g_after, g_before)
    g_far_a, g_far_b, near_after, near_before, fb = lax.optimization_barrier(
        (g_far_a, g_far_b, near_after, near_before, fb)
    )

    swap_far_a = lax.ppermute(g_far_a, "core", SWAP)
    swap_far_b = lax.ppermute(g_far_b, "core", SWAP)
    far_b = lax.ppermute(near_before, "z", ring(-1))
    gbuf_shape = jax.ShapeDtypeStruct((2, P_SIZE, COLS), jnp.bfloat16)
    fb, gbuf = pl.pallas_call(
        rest_kernel,
        out_shape=(fb_shape, gbuf_shape),
        in_specs=[smem_spec()] + [vmem_spec()] * 7 + [any_spec()] * 6,
        out_specs=(vmem_spec(), vmem_spec()),
        scratch_shapes=[
            pltpu.VMEM((2, 10 * SHARD, TILE), jnp.float32),
            pltpu.SemaphoreType.DMA((12,)),
        ],
        input_output_aliases={2: 0},
        compiler_params=pltpu.CompilerParams(vmem_limit_bytes=24 << 20),
        cost_estimate=pl.CostEstimate(flops=5 << 30, transcendentals=0, bytes_accessed=8 << 20),
        name="rest",
    )(
        state, abuf, fb, swap, g_far_a, g_far_b, swap_far_a, swap_far_b,
        own, near, after, before, near_after, near_before,
    )

    block = jax.ShapeDtypeStruct((N_CHIPS, 8, P_SIZE), jnp.bfloat16)
    _, keep, send = pl.pallas_call(
        finish_kernel,
        out_shape=(gbuf_shape, block, block),
        in_specs=[smem_spec(), vmem_spec(), vmem_spec(), any_spec(), any_spec()],
        out_specs=(vmem_spec(),) * 3,
        scratch_shapes=[pltpu.SemaphoreType.DMA((4,))],
        input_output_aliases={2: 0},
        compiler_params=pltpu.CompilerParams(vmem_limit_bytes=32 << 20),
        cost_estimate=pl.CostEstimate(flops=4 << 30, transcendentals=0, bytes_accessed=8 << 20),
        name="finish",
    )(state, fb, gbuf, far_a, far_b)
    taken = lax.ppermute(send, "core", SWAP)
    summed = (keep.astype(jnp.float32) + taken.astype(jnp.float32)).astype(jnp.bfloat16)
    parts = lax.all_to_all(summed, CHIPS, 0, 0)
    return pl.pallas_call(
        align_kernel,
        out_shape=jax.ShapeDtypeStruct((4, 2, P_SIZE), jnp.float32),
        in_specs=[smem_spec(), vmem_spec()],
        out_specs=vmem_spec(),
        name="align",
    )(reference_index, parts)


def solution(mesh):
    fine = Mesh(mesh.devices.reshape([size for _, size in PARTS]), [name for name, _ in PARTS])
    return jax.shard_map(
        body,
        mesh=fine,
        in_specs=(P(None, RCV, SRC), P(None, RCV, SRC), P(), P(ALL)),
        out_specs=P(ALL, None, None),
        check_vma=False,
    )
```

```python
import jax
import jax.numpy as jnp
from jax import lax
from jax.experimental import pallas as pl
from jax.experimental.pallas import tpu as pltpu
from jax.sharding import Mesh, PartitionSpec as P

P_SIZE = 512
TILE = 256
PARTS = (("xh", 2), ("z", 4), ("y", 4), ("xl", 2), ("core", 2))
RCV = ("xh", "z")
SRC = ("y", "xl", "core")
ALL = RCV + SRC
CHIPS = RCV + SRC[:2]
ROWS = 2048
COLS = 1024
ROW_TILES = ROWS // TILE
COL_TILES = COLS // TILE
SHARD = 32
N_CHIPS = 64
SWAP = [(0, 1), (1, 0)]


def place(xh, z, y, xl, core):
    return (((xh * 4 + z) * 4 + y) * 2 + xl) * 2 + core


def crossing(cross):
    return [
        (place(xh, z, y, xl, core), place(xl, y, 2 * xh + z // 2, z % 2, core ^ cross))
        for xh in range(2)
        for z in range(4)
        for y in range(4)
        for xl in range(2)
        for core in range(2)
    ]


def ring(step):
    return [(i, (i + step) % 4) for i in range(4)]


def dot(a, b):
    return lax.dot_general(a, b, (((1,), (0,)), ((), ())), preferred_element_type=jnp.float32)


def dot_nt(a, b):
    return lax.dot_general(a, b, (((1,), (1,)), ((), ())), preferred_element_type=jnp.float32)


def load_kernel(st, a, abuf, asem):
    def tile_copy(c, source, i):
        row = pl.multiple_of(source * TILE, TILE)
        return pltpu.make_async_copy(
            a.at[:, pl.ds(row, TILE), pl.ds(c * TILE, TILE)],
            abuf.at[c, :, pl.ds(i * TILE, TILE), :],
            asem.at[c, i],
        )

    def visit(act):
        for c in range(COL_TILES):
            for i in range(ROW_TILES):

                @pl.when(i < st[c])
                def _():
                    act(tile_copy(c, st[8 + c * ROW_TILES + i], i))

            @pl.when(st[40 + c] != 0)
            def _():
                act(tile_copy(c, st[44 + c], ROW_TILES))

    visit(lambda copy: copy.start())
    visit(lambda copy: copy.wait())


BLOCK = 2 * SHARD


def accumulators(blocks):
    return [pltpu.ACC(unit)((BLOCK, TILE), jnp.float32) for unit in range(2) for _ in range(blocks)]


def project(st, abuf, accs, saved, fb, left_of, targets):
    blocks = len(targets)

    def push(c, i):
        rows = pl.ds(pl.multiple_of(i * TILE, TILE), TILE)
        for unit in range(2):
            pltpu.matmul_push_rhs(abuf[c, unit, rows, :], 0, unit)

    def stream(t, after_first=None):
        left = left_of(t)
        for b in range(blocks):
            for unit in range(2):
                pltpu.matmul_acc_lhs(
                    accs[unit * blocks + b],
                    left[b * BLOCK : (b + 1) * BLOCK],
                    load_staged_rhs=0 if b == 0 else None,
                )
            if b == 0 and after_first:
                after_first()

    def column(c, carry):
        n = st[c]
        on_diag = st[40 + c] != 0
        lanes = pl.ds(pl.multiple_of(c * TILE, TILE), TILE)

        def popped(b):
            by_real = pltpu.matmul_pop(accs[b])
            by_imag = pltpu.matmul_pop(accs[blocks + b])
            return by_real[:SHARD], by_imag[:SHARD], by_real[SHARD:], by_imag[SHARD:]

        @pl.when(n > 0)
        def _():
            push(c, 0)

            def step(i, inner):
                stream(st[8 + c * ROW_TILES + i], lambda: push(c, i + 1))
                return inner

            lax.fori_loop(0, n - 1, step, 0)
            stream(st[8 + c * ROW_TILES + n - 1])

        def flush(save):
            for b, row in enumerate(targets):
                rows = pl.ds(pl.multiple_of(row, SHARD), SHARD)
                rr, ri, ir, ii = popped(b)
                fb[2, rows, lanes] = (rr - ii).astype(jnp.bfloat16)
                fb[3, rows, lanes] = (ri + ir).astype(jnp.bfloat16)
                if save:
                    saved[0, b * SHARD : (b + 1) * SHARD, :] = rr + ii
                    saved[1, b * SHARD : (b + 1) * SHARD, :] = ri - ir
                else:
                    fb[0, rows, lanes] = (rr + ii).astype(jnp.bfloat16)
                    fb[1, rows, lanes] = (ri - ir).astype(jnp.bfloat16)

        @pl.when(jnp.logical_not(on_diag))
        def _():
            flush(False)

        @pl.when(on_diag)
        def _():
            flush(True)
            push(c, ROW_TILES)
            stream(st[44 + c])
            for b, row in enumerate(targets):
                rows = pl.ds(pl.multiple_of(row, SHARD), SHARD)
                rr, ri, ir, ii = popped(b)
                at = slice(b * SHARD, (b + 1) * SHARD)
                fb[0, rows, lanes] = (saved[0, at, :] + (rr + ii)).astype(jnp.bfloat16)
                fb[1, rows, lanes] = (saved[1, at, :] + (ri - ir)).astype(jnp.bfloat16)

        return carry

    lax.fori_loop(0, COL_TILES, column, 0)


def line_row(st, x_other, y_step, other):
    core, xl, y = st[49], st[52], st[53]
    line = 4 * ((y + y_step + 4) % 4) + 2 * (1 - xl if x_other else xl)
    return (line + (1 - core if other else core)) * SHARD


def tile_lanes(t):
    return pl.ds(pl.multiple_of(t * TILE, TILE), TILE)


def near_kernel(st, abuf, own, after, before, fb, saved):
    @pl.when(st[48] != 0)
    def _():
        def left_of(t):
            return jnp.concatenate(
                [ref[:, :, :, tile_lanes(t)].reshape(4 * SHARD, TILE) for ref in (own, after, before)], axis=0
            )

        targets = [line_row(st, x, step, False) for step in (0, -1, 1) for x in range(2)]
        pl.run_scoped(
            lambda *accs: project(st, abuf, accs, saved, fb, left_of, targets), *accumulators(len(targets))
        )


def row_copies(st, gbuf, sem, pieces):
    core, xh, z = st[49], st[50], st[51]
    copies = []
    for ref, x_other, z_step in pieces:
        for part in range(2):
            block = 2 * ((z + z_step + 4) % 4) + (1 - xh if x_other else xh)
            slot = core if part == 0 else 1 - core
            row = pl.multiple_of(block * 64 + slot * SHARD, SHARD)
            target = gbuf.at[:, pl.ds(row, SHARD), :]
            copies.append(pltpu.make_async_copy(ref.at[part], target, sem.at[len(copies)]))
    return copies


def rest_kernel(
    st, abuf, fb_in, swap, g_far_a, g_far_b, swap_far_a, swap_far_b,
    own, near, after, before, near_after, near_before,
    fb, gbuf, saved, gsem,
):
    @pl.when(st[48] != 0)
    def _():
        copies = row_copies(
            st,
            gbuf,
            gsem,
            (
                (own, False, 0),
                (near, True, 0),
                (after, False, -1),
                (before, False, 1),
                (near_after, True, -1),
                (near_before, True, 1),
            ),
        )
        for copy in copies:
            copy.start()

        def left_of(t):
            lanes = tile_lanes(t)
            return jnp.concatenate(
                [
                    swap[:, :, :, :, lanes].reshape(12 * SHARD, TILE),
                ]
                + [
                    ref[:, :, lanes].reshape(2 * SHARD, TILE)
                    for ref in (g_far_a, g_far_b, swap_far_a, swap_far_b)
                ],
                axis=0,
            )

        targets = [line_row(st, x, step, True) for step in (0, -1, 1) for x in range(2)]
        targets += [line_row(st, x, 2, other) for other in (False, True) for x in range(2)]
        pl.run_scoped(
            lambda *accs: project(st, abuf, accs, saved, fb, left_of, targets), *accumulators(len(targets))
        )
        for copy in copies:
            copy.wait()


def finish_kernel(st, fb, gbuf_in, far_a, far_b, gbuf, keep, send, gsem):
    core = st[49]
    half = P_SIZE
    blocks = 2 * half // BLOCK
    chips = BLOCK // 8
    low = lax.broadcasted_iota(jnp.int32, (chips, 8, TILE), 1) < 4

    @pl.when(st[48] != 0)
    def _():
        copies = row_copies(st, gbuf, gsem, ((far_a, False, 2), (far_b, True, 2)))
        for copy in copies:
            copy.start()
        for copy in copies:
            copy.wait()

        steps = []
        for c in range(COL_TILES):
            cols = slice(c * TILE, (c + 1) * TILE)
            steps += [
                (lambda cols=cols: (fb[0, :, cols], fb[1, :, cols]), (gbuf, 0, cols)),
                (lambda cols=cols: (-fb[1, :, cols], fb[0, :, cols]), (gbuf, 1, cols)),
                (lambda cols=cols: (gbuf[0, :, cols], -gbuf[1, :, cols]), (fb, 2, cols)),
                (lambda cols=cols: (gbuf[1, :, cols], gbuf[0, :, cols]), (fb, 3, cols)),
            ]

        def push(step):
            ref, slot, cols = steps[step][1]
            for unit in range(2):
                right = ref[slot, unit * TILE : (unit + 1) * TILE, cols]
                pltpu.matmul_push_rhs(right, 0, unit, transpose=True)

        def multiply(*accs):
            push(0)
            for step in range(len(steps)):
                top, bottom = steps[step][0]()
                for b in range(blocks):
                    source = top if b < blocks // 2 else bottom
                    at = (b % (blocks // 2)) * BLOCK
                    for unit in range(2):
                        pltpu.matmul_acc_lhs(
                            accs[unit * blocks + b],
                            source[at : at + BLOCK],
                            load_staged_rhs=0 if b == 0 else None,
                        )
                    if b == 0 and step + 1 < len(steps):
                        push(step + 1)

            for b in range(blocks // 2):
                for unit in range(2):
                    re = pltpu.matmul_pop(accs[unit * blocks + b]).reshape(chips, 8, TILE)
                    im = pltpu.matmul_pop(accs[unit * blocks + blocks // 2 + b]).reshape(chips, 8, TILE)
                    first = jnp.where(low, re, pltpu.roll(im, 4, 1))
                    second = jnp.where(low, pltpu.roll(re, 4, 1), im)
                    at = slice(b * chips, (b + 1) * chips)
                    lanes = slice(unit * TILE, (unit + 1) * TILE)

                    keep[at, :, lanes] = jnp.where(core == 0, first, second).astype(jnp.bfloat16)
                    send[at, :, lanes] = jnp.where(core == 0, second, first).astype(jnp.bfloat16)

        pl.run_scoped(multiply, *accumulators(blocks))

    @pl.when(st[48] == 0)
    def _():
        keep[...] = jnp.zeros_like(keep)
        send[...] = jnp.zeros_like(send)


def align_kernel(index, parts, out):
    total = jnp.sum(parts[...].astype(jnp.float32), axis=0)
    re = total[:4]
    im = total[4:]
    row = lax.broadcasted_iota(jnp.int32, (4, P_SIZE), 0)
    target = jnp.where(row < 2, jnp.where(row == 0, index[0], index[1]), jnp.where(row == 2, index[2], index[3]))
    chosen = lax.broadcasted_iota(jnp.int32, (4, P_SIZE), 1) == target
    anchor_re = jnp.sum(jnp.where(chosen, re, 0.0), axis=1, keepdims=True)
    anchor_im = jnp.sum(jnp.where(chosen, im, 0.0), axis=1, keepdims=True)
    out[:, 0, :] = re * anchor_re + im * anchor_im
    out[:, 1, :] = im * anchor_re - re * anchor_im


def any_spec():
    return pl.BlockSpec(memory_space=pl.ANY)


def hbm_spec():
    return pl.BlockSpec(memory_space=pltpu.HBM)


def smem_spec():
    return pl.BlockSpec(memory_space=pltpu.SMEM)


def vmem_spec():
    return pl.BlockSpec(memory_space=pltpu.VMEM)


def tile_states(tile_mask):
    rcv = lax.axis_index(RCV)
    src = lax.axis_index(SRC)
    tiles = lax.dynamic_slice(tile_mask, (rcv * ROW_TILES, src * COL_TILES), (ROW_TILES, COL_TILES))
    kept = (tiles == 1).T
    rows = jnp.arange(ROW_TILES)[None, :]
    diag_row = jnp.arange(COL_TILES)[:, None] + src * COL_TILES - rcv * ROW_TILES
    diag = rows == diag_row
    plain = (kept & ~diag).astype(jnp.int32)
    count = jnp.sum(plain, axis=1)
    before = jnp.sum(plain[:, None, :] * (rows[0][None, :] < rows[0][:, None]), axis=2)
    hit = (before[:, None, :] == rows[0][None, :, None]) & (plain[:, None, :] == 1)
    order = jnp.sum(jnp.where(hit, rows[0][None, None, :], 0), axis=2)
    diag_on = jnp.sum((kept & diag).astype(jnp.int32), axis=1)
    diag_at = jnp.clip(diag_row[:, 0], 0, ROW_TILES - 1)
    scalars = jnp.stack(
        [jnp.max(kept.astype(jnp.int32))] + [lax.axis_index(name) for name in ("core", "xh", "z", "xl", "y")]
    )
    return jnp.concatenate(
        [count, jnp.zeros((4,), jnp.int32), order.reshape(-1), diag_on, diag_at, scalars]
    ).astype(jnp.int32)


def body(reflection, green, tile_mask, reference_index):
    lines = jnp.transpose(green, (0, 2, 1))
    state = tile_states(tile_mask)
    core = lax.axis_index("core")
    mid = ROWS // 2

    first = lax.optimization_barrier((core, state[48]))[0]
    same = lax.dynamic_slice_in_dim(lines, first * mid, mid, 2)
    other = lax.dynamic_slice_in_dim(lines, (1 - first) * mid, mid, 2)
    part_a = lax.ppermute(same, ALL, crossing(0))
    part_b = lax.ppermute(other, ALL, crossing(1))
    beside = lax.ppermute(lines, "xl", SWAP)

    g_own = jnp.stack([lines, beside])
    own = jnp.stack([part_a, part_b])
    g_after = lax.ppermute(g_own, "y", ring(1))
    g_before = lax.ppermute(g_own, "y", ring(-1))
    after = lax.ppermute(own, "z", ring(1))
    before = lax.ppermute(own, "z", ring(-1))
    near = lax.ppermute(own, "xh", SWAP)
    abuf_shape = jax.ShapeDtypeStruct((COL_TILES, 2, ROWS + TILE, TILE), jnp.bfloat16)
    fb_shape = jax.ShapeDtypeStruct((4, P_SIZE, COLS), jnp.bfloat16)
    abuf = pl.pallas_call(
        load_kernel,
        out_shape=abuf_shape,
        in_specs=[smem_spec(), hbm_spec()],
        out_specs=vmem_spec(),
        scratch_shapes=[pltpu.SemaphoreType.DMA((COL_TILES, ROW_TILES + 1))],
        compiler_params=pltpu.CompilerParams(vmem_limit_bytes=12 << 20),
        cost_estimate=pl.CostEstimate(flops=0, transcendentals=0, bytes_accessed=8 << 20),
        name="load",
    )(state, pltpu.with_memory_space_constraint(reflection, pltpu.HBM))
    abuf, near, after, before = lax.optimization_barrier((abuf, near, after, before))
    g_after, g_before, _, _ = lax.optimization_barrier((g_after, g_before, near, abuf))

    swap = lax.ppermute(jnp.stack([g_own, g_after, g_before]), "core", SWAP)
    g_far_a = lax.ppermute(g_after[0], "y", ring(1))
    g_far_b = lax.ppermute(g_before[1], "y", ring(-1))
    near_after = lax.ppermute(near, "z", ring(1))
    near_before = lax.ppermute(near, "z", ring(-1))
    far_a = lax.ppermute(after, "z", ring(1))
    fb = pl.pallas_call(
        near_kernel,
        out_shape=fb_shape,
        in_specs=[smem_spec()] + [vmem_spec()] * 4,
        out_specs=vmem_spec(),
        scratch_shapes=[pltpu.VMEM((2, 6 * SHARD, TILE), jnp.float32)],
        compiler_params=pltpu.CompilerParams(vmem_limit_bytes=24 << 20),
        cost_estimate=pl.CostEstimate(flops=3 << 30, transcendentals=0, bytes_accessed=8 << 20),
        name="near",
    )(state, abuf, g_own, g_after, g_before)
    g_far_a, g_far_b, near_after, near_before, fb = lax.optimization_barrier(
        (g_far_a, g_far_b, near_after, near_before, fb)
    )

    swap_far_a = lax.ppermute(g_far_a, "core", SWAP)
    swap_far_b = lax.ppermute(g_far_b, "core", SWAP)
    far_b = lax.ppermute(near_before, "z", ring(-1))
    gbuf_shape = jax.ShapeDtypeStruct((2, P_SIZE, COLS), jnp.bfloat16)
    fb, gbuf = pl.pallas_call(
        rest_kernel,
        out_shape=(fb_shape, gbuf_shape),
        in_specs=[smem_spec()] + [vmem_spec()] * 7 + [any_spec()] * 6,
        out_specs=(vmem_spec(), vmem_spec()),
        scratch_shapes=[
            pltpu.VMEM((2, 10 * SHARD, TILE), jnp.float32),
            pltpu.SemaphoreType.DMA((12,)),
        ],
        input_output_aliases={2: 0},
        compiler_params=pltpu.CompilerParams(vmem_limit_bytes=24 << 20),
        cost_estimate=pl.CostEstimate(flops=5 << 30, transcendentals=0, bytes_accessed=8 << 20),
        name="rest",
    )(
        state, abuf, fb, swap, g_far_a, g_far_b, swap_far_a, swap_far_b,
        own, near, after, before, near_after, near_before,
    )

    block = jax.ShapeDtypeStruct((N_CHIPS, 8, P_SIZE), jnp.bfloat16)
    _, keep, send = pl.pallas_call(
        finish_kernel,
        out_shape=(gbuf_shape, block, block),
        in_specs=[smem_spec(), vmem_spec(), vmem_spec(), any_spec(), any_spec()],
        out_specs=(vmem_spec(),) * 3,
        scratch_shapes=[pltpu.SemaphoreType.DMA((4,))],
        input_output_aliases={2: 0},
        compiler_params=pltpu.CompilerParams(vmem_limit_bytes=32 << 20),
        cost_estimate=pl.CostEstimate(flops=4 << 30, transcendentals=0, bytes_accessed=8 << 20),
        name="finish",
    )(state, fb, gbuf, far_a, far_b)
    taken = lax.ppermute(send, "core", SWAP)
    summed = (keep.astype(jnp.float32) + taken.astype(jnp.float32)).astype(jnp.bfloat16)
    parts = lax.all_to_all(summed, CHIPS, 0, 0)
    return pl.pallas_call(
        align_kernel,
        out_shape=jax.ShapeDtypeStruct((4, 2, P_SIZE), jnp.float32),
        in_specs=[smem_spec(), vmem_spec()],
        out_specs=vmem_spec(),
        name="align",
    )(reference_index, parts)


def solution(mesh):
    fine = Mesh(mesh.devices.reshape([size for _, size in PARTS]), [name for name, _ in PARTS])
    return jax.shard_map(
        body,
        mesh=fine,
        in_specs=(P(None, RCV, SRC), P(None, RCV, SRC), P(), P(ALL)),
        out_specs=P(ALL, None, None),
        check_vma=False,
    )
```

```python
import jax
import jax.numpy as jnp
from jax import lax
from jax.experimental import pallas as pl
from jax.experimental.pallas import tpu as pltpu
from jax.sharding import Mesh, PartitionSpec as P

P_SIZE = 512
TILE = 256
PARTS = (("xh", 2), ("z", 4), ("y", 4), ("xl", 2), ("core", 2))
RCV = ("xh", "z")
SRC = ("y", "xl", "core")
ALL = RCV + SRC
CHIPS = RCV + SRC[:2]
ROWS = 2048
COLS = 1024
ROW_TILES = ROWS // TILE
COL_TILES = COLS // TILE
SHARD = 32
N_CHIPS = 64
SWAP = [(0, 1), (1, 0)]


def place(xh, z, y, xl, core):
    return (((xh * 4 + z) * 4 + y) * 2 + xl) * 2 + core


def crossing(cross):
    return [
        (place(xh, z, y, xl, core), place(xl, y, 2 * xh + z // 2, z % 2, core ^ cross))
        for xh in range(2)
        for z in range(4)
        for y in range(4)
        for xl in range(2)
        for core in range(2)
    ]


def ring(step):
    return [(i, (i + step) % 4) for i in range(4)]


def dot(a, b):
    return lax.dot_general(a, b, (((1,), (0,)), ((), ())), preferred_element_type=jnp.float32)


def dot_nt(a, b):
    return lax.dot_general(a, b, (((1,), (1,)), ((), ())), preferred_element_type=jnp.float32)


def load_kernel(st, a, abuf, asem):
    def tile_copy(c, source, i):
        row = pl.multiple_of(source * TILE, TILE)
        return pltpu.make_async_copy(
            a.at[:, pl.ds(row, TILE), pl.ds(c * TILE, TILE)],
            abuf.at[c, :, pl.ds(i * TILE, TILE), :],
            asem.at[c, i],
        )

    def visit(act):
        for c in range(COL_TILES):
            for i in range(ROW_TILES):

                @pl.when(i < st[c])
                def _():
                    act(tile_copy(c, st[8 + c * ROW_TILES + i], i))

            @pl.when(st[40 + c] != 0)
            def _():
                act(tile_copy(c, st[44 + c], ROW_TILES))

    visit(lambda copy: copy.start())
    visit(lambda copy: copy.wait())


BLOCK = 2 * SHARD


def accumulators(blocks):
    return [pltpu.ACC(unit)((BLOCK, TILE), jnp.float32) for unit in range(2) for _ in range(blocks)]


def project(st, abuf, accs, saved, fb, left_of, targets):
    blocks = len(targets)

    def push(c, i):
        rows = pl.ds(pl.multiple_of(i * TILE, TILE), TILE)
        for unit in range(2):
            pltpu.matmul_push_rhs(abuf[c, unit, rows, :], 0, unit)

    def stream(t, after_first=None):
        left = left_of(t)
        for b in range(blocks):
            for unit in range(2):
                pltpu.matmul_acc_lhs(
                    accs[unit * blocks + b],
                    left[b * BLOCK : (b + 1) * BLOCK],
                    load_staged_rhs=0 if b == 0 else None,
                )
            if b == 0 and after_first:
                after_first()

    def column(c, carry):
        n = st[c]
        on_diag = st[40 + c] != 0
        lanes = pl.ds(pl.multiple_of(c * TILE, TILE), TILE)

        def popped(b):
            by_real = pltpu.matmul_pop(accs[b])
            by_imag = pltpu.matmul_pop(accs[blocks + b])
            return by_real[:SHARD], by_imag[:SHARD], by_real[SHARD:], by_imag[SHARD:]

        @pl.when(n > 0)
        def _():
            push(c, 0)

            def step(i, inner):
                stream(st[8 + c * ROW_TILES + i], lambda: push(c, i + 1))
                return inner

            lax.fori_loop(0, n - 1, step, 0)
            stream(st[8 + c * ROW_TILES + n - 1])

        def flush(save):
            for b, row in enumerate(targets):
                rows = pl.ds(pl.multiple_of(row, SHARD), SHARD)
                rr, ri, ir, ii = popped(b)
                fb[2, rows, lanes] = (rr - ii).astype(jnp.bfloat16)
                fb[3, rows, lanes] = (ri + ir).astype(jnp.bfloat16)
                if save:
                    saved[0, b * SHARD : (b + 1) * SHARD, :] = rr + ii
                    saved[1, b * SHARD : (b + 1) * SHARD, :] = ri - ir
                else:
                    fb[0, rows, lanes] = (rr + ii).astype(jnp.bfloat16)
                    fb[1, rows, lanes] = (ri - ir).astype(jnp.bfloat16)

        @pl.when(jnp.logical_not(on_diag))
        def _():
            flush(False)

        @pl.when(on_diag)
        def _():
            flush(True)
            push(c, ROW_TILES)
            stream(st[44 + c])
            for b, row in enumerate(targets):
                rows = pl.ds(pl.multiple_of(row, SHARD), SHARD)
                rr, ri, ir, ii = popped(b)
                at = slice(b * SHARD, (b + 1) * SHARD)
                fb[0, rows, lanes] = (saved[0, at, :] + (rr + ii)).astype(jnp.bfloat16)
                fb[1, rows, lanes] = (saved[1, at, :] + (ri - ir)).astype(jnp.bfloat16)

        return carry

    lax.fori_loop(0, COL_TILES, column, 0)


def line_row(st, x_other, y_step, other):
    core, xl, y = st[49], st[52], st[53]
    line = 4 * ((y + y_step + 4) % 4) + 2 * (1 - xl if x_other else xl)
    return (line + (1 - core if other else core)) * SHARD


def tile_lanes(t):
    return pl.ds(pl.multiple_of(t * TILE, TILE), TILE)


def near_kernel(st, abuf, own, after, before, fb, saved):
    @pl.when(st[48] != 0)
    def _():
        def left_of(t):
            return jnp.concatenate(
                [ref[:, :, :, tile_lanes(t)].reshape(4 * SHARD, TILE) for ref in (own, after, before)], axis=0
            )

        targets = [line_row(st, x, step, False) for step in (0, -1, 1) for x in range(2)]
        pl.run_scoped(
            lambda *accs: project(st, abuf, accs, saved, fb, left_of, targets), *accumulators(len(targets))
        )


def row_copies(st, gbuf, sem, pieces):
    core, xh, z = st[49], st[50], st[51]
    copies = []
    for ref, x_other, z_step in pieces:
        for part in range(2):
            block = 2 * ((z + z_step + 4) % 4) + (1 - xh if x_other else xh)
            slot = core if part == 0 else 1 - core
            row = pl.multiple_of(block * 64 + slot * SHARD, SHARD)
            target = gbuf.at[:, pl.ds(row, SHARD), :]
            copies.append(pltpu.make_async_copy(ref.at[part], target, sem.at[len(copies)]))
    return copies


def rest_kernel(
    st, abuf, fb_in, swap, g_far_a, g_far_b, swap_far_a, swap_far_b,
    own, near, after, before, near_after, near_before,
    fb, gbuf, saved, gsem,
):
    @pl.when(st[48] != 0)
    def _():
        copies = row_copies(
            st,
            gbuf,
            gsem,
            (
                (own, False, 0),
                (near, True, 0),
                (after, False, -1),
                (before, False, 1),
                (near_after, True, -1),
                (near_before, True, 1),
            ),
        )
        for copy in copies:
            copy.start()

        def left_of(t):
            lanes = tile_lanes(t)
            return jnp.concatenate(
                [
                    swap[:, :, :, :, lanes].reshape(12 * SHARD, TILE),
                ]
                + [
                    ref[:, :, lanes].reshape(2 * SHARD, TILE)
                    for ref in (g_far_a, g_far_b, swap_far_a, swap_far_b)
                ],
                axis=0,
            )

        targets = [line_row(st, x, step, True) for step in (0, -1, 1) for x in range(2)]
        targets += [line_row(st, x, 2, other) for other in (False, True) for x in range(2)]
        pl.run_scoped(
            lambda *accs: project(st, abuf, accs, saved, fb, left_of, targets), *accumulators(len(targets))
        )
        for copy in copies:
            copy.wait()


def finish_kernel(st, fb, gbuf_in, far_a, far_b, gbuf, keep, send, gsem):
    core = st[49]
    half = P_SIZE
    blocks = 2 * half // BLOCK
    chips = BLOCK // 8
    low = lax.broadcasted_iota(jnp.int32, (chips, 8, TILE), 1) < 4

    @pl.when(st[48] != 0)
    def _():
        copies = row_copies(st, gbuf, gsem, ((far_a, False, 2), (far_b, True, 2)))
        for copy in copies:
            copy.start()
        for copy in copies:
            copy.wait()

        steps = []
        for c in range(COL_TILES):
            cols = slice(c * TILE, (c + 1) * TILE)
            steps += [
                (lambda cols=cols: (fb[0, :, cols], fb[1, :, cols]), (gbuf, 0, cols)),
                (lambda cols=cols: (-fb[1, :, cols], fb[0, :, cols]), (gbuf, 1, cols)),
                (lambda cols=cols: (gbuf[0, :, cols], -gbuf[1, :, cols]), (fb, 2, cols)),
                (lambda cols=cols: (gbuf[1, :, cols], gbuf[0, :, cols]), (fb, 3, cols)),
            ]

        def push(step):
            ref, slot, cols = steps[step][1]
            for unit in range(2):
                right = ref[slot, unit * TILE : (unit + 1) * TILE, cols]
                pltpu.matmul_push_rhs(right, 0, unit, transpose=True)

        def multiply(*accs):
            push(0)
            for step in range(len(steps)):
                top, bottom = steps[step][0]()
                for b in range(blocks):
                    source = top if b < blocks // 2 else bottom
                    at = (b % (blocks // 2)) * BLOCK
                    for unit in range(2):
                        pltpu.matmul_acc_lhs(
                            accs[unit * blocks + b],
                            source[at : at + BLOCK],
                            load_staged_rhs=0 if b == 0 else None,
                        )
                    if b == 0 and step + 1 < len(steps):
                        push(step + 1)

            for b in range(blocks // 2):
                for unit in range(2):
                    re = pltpu.matmul_pop(accs[unit * blocks + b]).reshape(chips, 8, TILE)
                    im = pltpu.matmul_pop(accs[unit * blocks + blocks // 2 + b]).reshape(chips, 8, TILE)
                    first = jnp.where(low, re, pltpu.roll(im, 4, 1))
                    second = jnp.where(low, pltpu.roll(re, 4, 1), im)
                    at = slice(b * chips, (b + 1) * chips)
                    lanes = slice(unit * TILE, (unit + 1) * TILE)

                    keep[at, :, lanes] = jnp.where(core == 0, first, second).astype(jnp.bfloat16)
                    send[at, :, lanes] = jnp.where(core == 0, second, first).astype(jnp.bfloat16)

        pl.run_scoped(multiply, *accumulators(blocks))

    @pl.when(st[48] == 0)
    def _():
        keep[...] = jnp.zeros_like(keep)
        send[...] = jnp.zeros_like(send)


def align_kernel(index, parts, out):
    total = jnp.sum(parts[...].astype(jnp.float32), axis=0)
    re = total[:4]
    im = total[4:]
    chosen = lax.broadcasted_iota(jnp.int32, (4, P_SIZE), 1) == index[:, 0:1]
    anchor_re = jnp.sum(jnp.where(chosen, re, 0.0), axis=1, keepdims=True)
    anchor_im = jnp.sum(jnp.where(chosen, im, 0.0), axis=1, keepdims=True)
    out[:, 0, :] = re * anchor_re + im * anchor_im
    out[:, 1, :] = im * anchor_re - re * anchor_im


def any_spec():
    return pl.BlockSpec(memory_space=pl.ANY)


def hbm_spec():
    return pl.BlockSpec(memory_space=pltpu.HBM)


def smem_spec():
    return pl.BlockSpec(memory_space=pltpu.SMEM)


def vmem_spec():
    return pl.BlockSpec(memory_space=pltpu.VMEM)


def tile_states(tile_mask):
    rcv = lax.axis_index(RCV)
    src = lax.axis_index(SRC)
    tiles = lax.dynamic_slice(tile_mask, (rcv * ROW_TILES, src * COL_TILES), (ROW_TILES, COL_TILES))
    kept = (tiles == 1).T
    rows = jnp.arange(ROW_TILES)[None, :]
    diag_row = jnp.arange(COL_TILES)[:, None] + src * COL_TILES - rcv * ROW_TILES
    diag = rows == diag_row
    plain = (kept & ~diag).astype(jnp.int32)
    count = jnp.sum(plain, axis=1)
    before = jnp.sum(plain[:, None, :] * (rows[0][None, :] < rows[0][:, None]), axis=2)
    hit = (before[:, None, :] == rows[0][None, :, None]) & (plain[:, None, :] == 1)
    order = jnp.sum(jnp.where(hit, rows[0][None, None, :], 0), axis=2)
    diag_on = jnp.sum((kept & diag).astype(jnp.int32), axis=1)
    diag_at = jnp.clip(diag_row[:, 0], 0, ROW_TILES - 1)
    scalars = jnp.stack(
        [jnp.max(kept.astype(jnp.int32))] + [lax.axis_index(name) for name in ("core", "xh", "z", "xl", "y")]
    )
    return jnp.concatenate(
        [count, jnp.zeros((4,), jnp.int32), order.reshape(-1), diag_on, diag_at, scalars]
    ).astype(jnp.int32)


def body(reflection, green, tile_mask, reference_index):
    lines = jnp.transpose(green, (0, 2, 1))
    state = tile_states(tile_mask)
    core = lax.axis_index("core")
    mid = ROWS // 2

    first = lax.optimization_barrier((core, state[48]))[0]
    same = lax.dynamic_slice_in_dim(lines, first * mid, mid, 2)
    other = lax.dynamic_slice_in_dim(lines, (1 - first) * mid, mid, 2)
    part_a = lax.ppermute(same, ALL, crossing(0))
    part_b = lax.ppermute(other, ALL, crossing(1))
    beside = lax.ppermute(lines, "xl", SWAP)

    g_own = jnp.stack([lines, beside])
    own = jnp.stack([part_a, part_b])
    g_after = lax.ppermute(g_own, "y", ring(1))
    g_before = lax.ppermute(g_own, "y", ring(-1))
    after = lax.ppermute(own, "z", ring(1))
    before = lax.ppermute(own, "z", ring(-1))
    near = lax.ppermute(own, "xh", SWAP)
    abuf_shape = jax.ShapeDtypeStruct((COL_TILES, 2, ROWS + TILE, TILE), jnp.bfloat16)
    fb_shape = jax.ShapeDtypeStruct((4, P_SIZE, COLS), jnp.bfloat16)
    abuf = pl.pallas_call(
        load_kernel,
        out_shape=abuf_shape,
        in_specs=[smem_spec(), hbm_spec()],
        out_specs=vmem_spec(),
        scratch_shapes=[pltpu.SemaphoreType.DMA((COL_TILES, ROW_TILES + 1))],
        compiler_params=pltpu.CompilerParams(vmem_limit_bytes=12 << 20),
        cost_estimate=pl.CostEstimate(flops=0, transcendentals=0, bytes_accessed=8 << 20),
        name="load",
    )(state, pltpu.with_memory_space_constraint(reflection, pltpu.HBM))
    abuf, near, after, before = lax.optimization_barrier((abuf, near, after, before))
    g_after, g_before, _, _ = lax.optimization_barrier((g_after, g_before, near, abuf))

    swap = lax.ppermute(jnp.stack([g_own, g_after, g_before]), "core", SWAP)
    g_far_a = lax.ppermute(g_after[0], "y", ring(1))
    g_far_b = lax.ppermute(g_before[1], "y", ring(-1))
    near_after = lax.ppermute(near, "z", ring(1))
    near_before = lax.ppermute(near, "z", ring(-1))
    far_a = lax.ppermute(after, "z", ring(1))
    fb = pl.pallas_call(
        near_kernel,
        out_shape=fb_shape,
        in_specs=[smem_spec()] + [vmem_spec()] * 4,
        out_specs=vmem_spec(),
        scratch_shapes=[pltpu.VMEM((2, 6 * SHARD, TILE), jnp.float32)],
        compiler_params=pltpu.CompilerParams(vmem_limit_bytes=24 << 20),
        cost_estimate=pl.CostEstimate(flops=3 << 30, transcendentals=0, bytes_accessed=8 << 20),
        name="near",
    )(state, abuf, g_own, g_after, g_before)
    g_far_a, g_far_b, near_after, near_before, fb = lax.optimization_barrier(
        (g_far_a, g_far_b, near_after, near_before, fb)
    )

    swap_far_a = lax.ppermute(g_far_a, "core", SWAP)
    swap_far_b = lax.ppermute(g_far_b, "core", SWAP)
    far_b = lax.ppermute(near_before, "z", ring(-1))
    gbuf_shape = jax.ShapeDtypeStruct((2, P_SIZE, COLS), jnp.bfloat16)
    fb, gbuf = pl.pallas_call(
        rest_kernel,
        out_shape=(fb_shape, gbuf_shape),
        in_specs=[smem_spec()] + [vmem_spec()] * 7 + [any_spec()] * 6,
        out_specs=(vmem_spec(), vmem_spec()),
        scratch_shapes=[
            pltpu.VMEM((2, 10 * SHARD, TILE), jnp.float32),
            pltpu.SemaphoreType.DMA((12,)),
        ],
        input_output_aliases={2: 0},
        compiler_params=pltpu.CompilerParams(vmem_limit_bytes=24 << 20),
        cost_estimate=pl.CostEstimate(flops=5 << 30, transcendentals=0, bytes_accessed=8 << 20),
        name="rest",
    )(
        state, abuf, fb, swap, g_far_a, g_far_b, swap_far_a, swap_far_b,
        own, near, after, before, near_after, near_before,
    )

    block = jax.ShapeDtypeStruct((N_CHIPS, 8, P_SIZE), jnp.bfloat16)
    _, keep, send = pl.pallas_call(
        finish_kernel,
        out_shape=(gbuf_shape, block, block),
        in_specs=[smem_spec(), vmem_spec(), vmem_spec(), any_spec(), any_spec()],
        out_specs=(vmem_spec(),) * 3,
        scratch_shapes=[pltpu.SemaphoreType.DMA((4,))],
        input_output_aliases={2: 0},
        compiler_params=pltpu.CompilerParams(vmem_limit_bytes=32 << 20),
        cost_estimate=pl.CostEstimate(flops=4 << 30, transcendentals=0, bytes_accessed=8 << 20),
        name="finish",
    )(state, fb, gbuf, far_a, far_b)
    taken = lax.ppermute(send, "core", SWAP)
    summed = (keep.astype(jnp.float32) + taken.astype(jnp.float32)).astype(jnp.bfloat16)
    parts = lax.all_to_all(summed, CHIPS, 0, 0)
    return pl.pallas_call(
        align_kernel,
        out_shape=jax.ShapeDtypeStruct((4, 2, P_SIZE), jnp.float32),
        in_specs=[vmem_spec(), vmem_spec()],
        out_specs=vmem_spec(),
        name="align",
    )(jnp.broadcast_to(reference_index[:, None], (4, 128)), parts)


def solution(mesh):
    fine = Mesh(mesh.devices.reshape([size for _, size in PARTS]), [name for name, _ in PARTS])
    return jax.shard_map(
        body,
        mesh=fine,
        in_specs=(P(None, RCV, SRC), P(None, RCV, SRC), P(), P(ALL)),
        out_specs=P(ALL, None, None),
        check_vma=False,
    )
```
